32 devices in a mesh: dp: 8 (over z, y), head: 4 (over x, core).
Axes of the slice: x: 2, y: 2, z: 4, core: 2. Of those that a mesh axis runs over, the one named last changes fastest.
Arguments:
- features: float32 [2, 8, 768, 128], P(None, 'dp'), may hold values from -6 to 6
- targets: float32 [2, 8, 768], P(None, 'dp'), may hold values from -6 to 6
- neighbours: int32 [2, 8, 256, 256], P(None, 'dp'), may hold values from 0 to 511, as said below
- nbr_mask: int32 [2, 8, 256, 256], P(None, 'dp'), may hold values from 0 to 1, as said below
- flags: int32 [2, 8, 256], P(None, 'dp'), may hold values 0 or 1
- step_count: int32 [1], replicated, may hold values from 2 to 20
- w_qkv: float32 [2, 768, 2304], P(None, 'dp', 'head'), may hold values from -0.21875 to 0.21875
- w_out: float32 [2, 768, 768], P(None, 'dp', 'head'), may hold values from -0.875 to 0.875
- w_up: float32 [2, 768, 3072], P(None, 'dp', 'head'), may hold values from -0.21875 to 0.21875
- w_down: float32 [2, 768, 3072], P(None, 'dp', 'head'), may hold values from -0.109375 to 0.109375
- emb_weight: float32 [768, 128], P('dp'), may hold values from -0.5 to 0.5
- vectors: float32 [768, 7], P('dp'), may hold values from -4 to 4
- m_qkv: float32 [2, 768, 2304], P(None, 'dp', 'head'), may hold values from -7.6293945e-06 to 7.6293945e-06
- m_out: float32 [2, 768, 768], P(None, 'dp', 'head'), may hold values from -7.6293945e-06 to 7.6293945e-06
- m_up: float32 [2, 768, 3072], P(None, 'dp', 'head'), may hold values from -7.6293945e-06 to 7.6293945e-06
- m_down: float32 [2, 768, 3072], P(None, 'dp', 'head'), may hold values from -7.6293945e-06 to 7.6293945e-06
- m_emb: float32 [768, 128], P('dp'), may hold values from -7.6293945e-06 to 7.6293945e-06
- m_vectors: float32 [768, 7], P('dp'), may hold values from -9.1552734e-05 to 9.1552734e-05
- v_qkv: float32 [2, 768, 2304], P(None, 'dp', 'head'), may hold values from 2.8051561e-14 to 1.12206244e-13
- v_out: float32 [2, 768, 768], P(None, 'dp', 'head'), may hold values from 2.8051561e-14 to 1.12206244e-13
- v_up: float32 [2, 768, 3072], P(None, 'dp', 'head'), may hold values from 2.8051561e-14 to 1.12206244e-13
- v_down: float32 [2, 768, 3072], P(None, 'dp', 'head'), may hold values from 2.8051561e-14 to 1.12206244e-13
- v_emb: float32 [768, 128], P('dp'), may hold values from 2.8051561e-14 to 1.12206244e-13
- v_vectors: float32 [768, 7], P('dp'), may hold values from 2.805156e-12 to 1.1220624e-11
Outputs:
- loss: float32 [], replicated
- grad_norm: float32 [], replicated
- new_qkv: float32 [2, 768, 2304], P(None, 'dp', 'head')
- new_out: float32 [2, 768, 768], P(None, 'dp', 'head')
- new_up: float32 [2, 768, 3072], P(None, 'dp', 'head')
- new_down: float32 [2, 768, 3072], P(None, 'dp', 'head')
- new_emb: float32 [768, 128], P('dp')
- new_vectors: float32 [768, 7], P('dp')
- nm_qkv: float32 [2, 768, 2304], P(None, 'dp', 'head')
- nm_out: float32 [2, 768, 768], P(None, 'dp', 'head')
- nm_up: float32 [2, 768, 3072], P(None, 'dp', 'head')
- nm_down: float32 [2, 768, 3072], P(None, 'dp', 'head')
- nm_emb: float32 [768, 128], P('dp')
- nm_vectors: float32 [768, 7], P('dp')
- nv_qkv: float32 [2, 768, 2304], P(None, 'dp', 'head')
- nv_out: float32 [2, 768, 768], P(None, 'dp', 'head')
- nv_up: float32 [2, 768, 3072], P(None, 'dp', 'head')
- nv_down: float32 [2, 768, 3072], P(None, 'dp', 'head')
- nv_emb: float32 [768, 128], P('dp')
- nv_vectors: float32 [768, 7], P('dp')
The draws below stay inside these ranges and needn't reach their ends.
Inputs may be any that keep to these rules, and one draw needn't show every extreme that they name: `neighbours`: the 256 indices of one query row are distinct. `nbr_mask`: slot 0 of every query row is live.
All inputs are finite; a program needn't handle non-finite values. No bound on the sum of `flags` on one device may be relied on, other than what follows from the above.
Results may differ from the reference program's by a relative error of at most 0.0003.
Values sent between devices are 32-bit elements; how exact they have to be, the bound alone decides.
No kernel may reach another device: no remote copies, remote signals or barrier semaphores. Data moves between devices by JAX's collectives and lax.ppermute only.
A program may use at most 256 MiB of HBM per device.

```python
import math
import jax
import jax.numpy as jnp
from jax import lax

D = 768
HD = 64
FF = 3072
F = 128
NL = 2
MB = 2
CTX = 512
KNN = 256
QRY = 256
ROWS = 768
TABLES = 8
HEADS = 12
NV = 7
P_ALL = 14259456
N_HEAD = 4


def draw_neighbours(key, part):
    keys = jax.random.split(key, MB * TABLES * QRY)
    picked = jax.vmap(lambda single: jax.random.permutation(single, CTX)[:KNN])(keys)
    return picked.reshape(MB, TABLES, QRY, KNN).astype(jnp.int32)


def draw_nbr_mask(key, part):
    coins = jax.random.randint(key, (MB, TABLES, QRY, KNN), 0, 8)
    slots = jnp.arange(KNN)[None, None, None, :]
    return jnp.where(slots == 0, 1, (coins > 0).astype(jnp.int32)).astype(jnp.int32)


def draw_vectors(key, part):
    base = jnp.clip(jax.random.normal(key, (D, NV), jnp.float32), -4.0, 4.0)
    column = jnp.arange(NV)[None, :] + jnp.zeros((D, 1), jnp.int32)
    gains = 1.0 + 0.1 * base
    head = base * D ** (-0.5)
    result = jnp.where(column <= 2 * NL, gains, jnp.where(column == 2 * NL + 1, base, head))
    return result.astype(jnp.float32)


def with_ends(entries, own_key, low, top_value):
    extent = entries.shape
    place = [jax.random.randint(jax.random.fold_in(own_key, axis), (), 0, extent[axis]) for axis in range(len(extent))]
    entries = entries.at[tuple(place)].set(low)
    longest = extent.index(max(extent))
    place[longest] = (place[longest] + 1) % extent[longest]
    return entries.at[tuple(place)].set(top_value)


def block_scale(own_key, dims, pieces, least, high):
    level, own = 1.0, jax.random.fold_in(own_key, 6)
    for dim, parts in pieces:
        steps = jnp.exp(jax.random.uniform(jax.random.fold_in(own, dim), (parts,), jnp.float32, least / len(pieces), high / len(pieces)))
        level = level * jnp.repeat(steps, dims[dim] // parts).reshape([-1 if axis == dim else 1 for axis in range(len(dims))])
    return level


def gaussian(rng, dims, scale, reach, cuts=(), held_as=jnp.bfloat16):
    values = jax.random.normal(rng, dims, jnp.float32) * scale
    if len(cuts) > 0:
        values = block_scale(rng, dims, cuts, -0.22, 0.18) * values
    return jnp.clip(values, min=-reach, max=reach).astype(held_as)


def setup_inputs(seed: int = 0) -> dict:
    streams_of = jax.random.split(jax.random.key(seed), 25)
    features = gaussian(streams_of[0], (MB, TABLES, ROWS, F), 1.0, 6.0, ((1, 8),), jnp.float32)
    targets = gaussian(streams_of[1], (MB, TABLES, ROWS), 1.0, 6.0, ((1, 8),), jnp.float32)
    neighbours = draw_neighbours(jax.random.fold_in(streams_of[24], 71), 0)
    nbr_mask = draw_nbr_mask(jax.random.fold_in(streams_of[24], 71), 0)
    flags = with_ends((jax.random.randint(streams_of[4], (MB, TABLES, QRY), 0, 4) < 3).astype(jnp.int32), jax.random.fold_in(streams_of[4], 1), 0, 1)
    step_count = jax.random.randint(streams_of[5], (1,), 2, 21).astype(jnp.int32)
    w_qkv = gaussian(streams_of[6], (NL, D, 3 * D), D ** -0.5, 0.21875, ((1, 8), (2, 4)), jnp.float32)
    w_out = gaussian(streams_of[7], (NL, D, D), (D // 16) ** -0.5, 0.875, ((1, 8), (2, 4)), jnp.float32)
    w_up = gaussian(streams_of[8], (NL, D, FF), D ** -0.5, 0.21875, ((1, 8), (2, 4)), jnp.float32)
    w_down = gaussian(streams_of[9], (NL, D, FF), FF ** -0.5, 0.109375, ((1, 8), (2, 4)), jnp.float32)
    emb_weight = gaussian(streams_of[10], (D, F), F ** -0.5, 0.5, ((0, 8),), jnp.float32)
    vectors = draw_vectors(jax.random.fold_in(streams_of[24], 71), 0)
    m_qkv = gaussian(streams_of[12], (NL, D, 3 * D), (0.111 * 0.02 / P_ALL ** 0.5), 7.62939453125e-06, ((1, 8), (2, 4)), jnp.float32)
    m_out = gaussian(streams_of[13], (NL, D, D), (0.111 * 0.02 / P_ALL ** 0.5), 7.62939453125e-06, ((1, 8), (2, 4)), jnp.float32)
    m_up = gaussian(streams_of[14], (NL, D, FF), (0.111 * 0.02 / P_ALL ** 0.5), 7.62939453125e-06, ((1, 8), (2, 4)), jnp.float32)
    m_down = gaussian(streams_of[15], (NL, D, FF), (0.111 * 0.02 / P_ALL ** 0.5), 7.62939453125e-06, ((1, 8), (2, 4)), jnp.float32)
    m_emb = gaussian(streams_of[16], (D, F), (0.111 * 0.02 / P_ALL ** 0.5), 7.62939453125e-06, ((0, 8),), jnp.float32)
    m_vectors = gaussian(streams_of[17], (D, NV), (1.11 * 0.02 / P_ALL ** 0.5), 9.1552734375e-05, ((0, 8),), jnp.float32)
    v_qkv = jnp.clip(jnp.exp(math.log(1.1220624445860625e-13) - 1.3862944 * jax.random.uniform(streams_of[18], (NL, D, 3 * D), jnp.float32) ** block_scale(streams_of[18], (NL, D, 3 * D), ((1, 8), (2, 4)), -0.2, 0.2)), 2.8051561114651562e-14, 1.1220624445860625e-13)
    v_out = jnp.clip(jnp.exp(math.log(1.1220624445860625e-13) - 1.3862944 * jax.random.uniform(streams_of[19], (NL, D, D), jnp.float32) ** block_scale(streams_of[19], (NL, D, D), ((1, 8), (2, 4)), -0.2, 0.2)), 2.8051561114651562e-14, 1.1220624445860625e-13)
    v_up = jnp.clip(jnp.exp(math.log(1.1220624445860625e-13) - 1.3862944 * jax.random.uniform(streams_of[20], (NL, D, FF), jnp.float32) ** block_scale(streams_of[20], (NL, D, FF), ((1, 8), (2, 4)), -0.2, 0.2)), 2.8051561114651562e-14, 1.1220624445860625e-13)
    v_down = jnp.clip(jnp.exp(math.log(1.1220624445860625e-13) - 1.3862944 * jax.random.uniform(streams_of[21], (NL, D, FF), jnp.float32) ** block_scale(streams_of[21], (NL, D, FF), ((1, 8), (2, 4)), -0.2, 0.2)), 2.8051561114651562e-14, 1.1220624445860625e-13)
    v_emb = jnp.clip(jnp.exp(math.log(1.1220624445860625e-13) - 1.3862944 * jax.random.uniform(streams_of[22], (D, F), jnp.float32) ** block_scale(streams_of[22], (D, F), ((0, 8),), -0.2, 0.2)), 2.8051561114651562e-14, 1.1220624445860625e-13)
    v_vectors = jnp.clip(jnp.exp(math.log(1.1220624256125245e-11) - 1.3862944 * jax.random.uniform(streams_of[23], (D, NV), jnp.float32) ** block_scale(streams_of[23], (D, NV), ((0, 8),), -0.2, 0.2)), 2.805156064031311e-12, 1.1220624256125245e-11)
    return {"features": features, "targets": targets, "neighbours": neighbours, "nbr_mask": nbr_mask, "flags": flags, "step_count": step_count, "w_qkv": w_qkv, "w_out": w_out, "w_up": w_up, "w_down": w_down, "emb_weight": emb_weight, "vectors": vectors, "m_qkv": m_qkv, "m_out": m_out, "m_up": m_up, "m_down": m_down, "m_emb": m_emb, "m_vectors": m_vectors, "v_qkv": v_qkv, "v_out": v_out, "v_up": v_up, "v_down": v_down, "v_emb": v_emb, "v_vectors": v_vectors}


HIGHEST = lax.Precision.HIGHEST
LR_MATRIX = 0.03
LR_VECTOR = 0.2
DECAY = 0.1
CLIP_AT = 0.02

@jax.custom_vjp
def low(v):
    return lax.optimization_barrier(v.astype(jnp.bfloat16)).astype(jnp.float32)

@jax.custom_vjp
def low_back(v):
    return v

def low_keep(v):
    return (low(v), None)

def low_pass(kept, grad):
    return (grad,)

def back_keep(v):
    return (v, None)

def back_low(kept, grad):
    return (low(grad),)
low.defvjp(low_keep, low_pass)
low_back.defvjp(back_keep, back_low)

def matmul(left, right):
    return jnp.dot(left, right, precision=HIGHEST, preferred_element_type=jnp.float32)

def norm_rows(values, gain):
    centre = values - lax.optimization_barrier(jnp.mean(values, axis=-1, keepdims=True))
    spread = lax.optimization_barrier(jnp.mean(centre * centre, axis=-1, keepdims=True))
    return centre * lax.rsqrt(spread + 1e-05) * gain

def gelu_tanh(values):
    return 0.5 * values * (1.0 + jnp.tanh(0.7978845608 * (values + 0.044715 * values * values * values)))

def allowed_rows(neigh, live):
    picks = jnp.zeros((QRY, CTX), jnp.float32)
    picks = picks.at[jnp.arange(QRY)[:, None], neigh].max(live.astype(jnp.float32))
    return jnp.concatenate([jnp.ones((CTX, CTX), jnp.float32), picks], axis=0)

def attend(query, keys, values, allowed):
    scores = jnp.einsum('rhe,che->hrc', query, keys, precision=HIGHEST) * HD ** (-0.5)
    masked = jnp.where(allowed[None] > 0, scores, -1e+30)
    top = lax.optimization_barrier(jnp.max(masked, axis=2, keepdims=True))
    expo = jnp.exp(masked - top)
    probs = expo / lax.optimization_barrier(jnp.sum(expo, axis=2, keepdims=True))
    return jnp.einsum('hrc,che->rhe', probs, values, precision=HIGHEST)

def table_loss(params, feat, target, neigh, live, flag):
    w_qkv, w_out, w_up, w_down, emb_weight, vectors = params
    is_context = (jnp.arange(ROWS) < CTX).astype(jnp.float32)
    hidden = matmul(feat, emb_weight.T) + (is_context * target)[:, None] * vectors[:, 2 * NL + 1][None, :]
    allowed = allowed_rows(neigh, live)
    for layer_idx in range(NL):
        normed = norm_rows(hidden, vectors[:, layer_idx])
        packed = matmul(normed, w_qkv[layer_idx]).reshape(ROWS, N_HEAD, 3, HEADS // N_HEAD, HD)
        query = packed[:, :, 0].reshape(ROWS, HEADS, HD)
        keys = packed[:CTX, :, 1].reshape(CTX, HEADS, HD)
        values = packed[:CTX, :, 2].reshape(CTX, HEADS, HD)
        mixed = attend(query, keys, values, allowed).reshape(ROWS, D)
        hidden = hidden + matmul(mixed, w_out[layer_idx].T)
        normed = norm_rows(hidden, vectors[:, NL + layer_idx])
        hidden = hidden + matmul(gelu_tanh(matmul(normed, w_up[layer_idx])), w_down[layer_idx].T)
    final = norm_rows(hidden[CTX:], vectors[:, 2 * NL])
    predicted = matmul(final, vectors[:, 2 * NL + 2])
    error = predicted - target[CTX:]
    return jnp.sum(flag * error * error)

def adamw(weight, grad, first, second, rate, decay, steps_taken):
    first_new = 0.9 * first + 0.1 * grad
    second_new = 0.999 * second + 0.001 * grad * grad
    first_hat = first_new / (1.0 - jnp.power(0.9, steps_taken))
    second_hat = second_new / (1.0 - jnp.power(0.999, steps_taken))
    weight_new = weight - rate * (first_hat / (jnp.sqrt(second_hat) + 1e-08) + decay * weight)
    return (weight_new, first_new, second_new)

def reference(features, targets, neighbours, nbr_mask, flags, step_count, w_qkv, w_out, w_up, w_down, emb_weight, vectors, m_qkv, m_out, m_up, m_down, m_emb, m_vectors, v_qkv, v_out, v_up, v_down, v_emb, v_vectors):
    params = (w_qkv, w_out, w_up, w_down, emb_weight, vectors)
    flag_all = flags.astype(jnp.float32).reshape(MB * TABLES, QRY)
    counted = jnp.maximum(jnp.sum(flag_all), 1.0)
    items = (features.reshape(MB * TABLES, ROWS, F), targets.reshape(MB * TABLES, ROWS), neighbours.reshape(MB * TABLES, QRY, KNN).astype(jnp.int32), nbr_mask.reshape(MB * TABLES, QRY, KNN), flag_all)
    checked = jax.checkpoint(table_loss)

    def total(weights):

        def one(carry, item):
            feat, target, neigh, live, flag = item
            return (carry + checked(weights, feat, target, neigh, live, flag), None)
        summed, unused = lax.scan(one, jnp.zeros((), jnp.float32), items)
        return summed / counted
    loss, pull = jax.vjp(total, params)
    grads = pull(jnp.ones((), jnp.float32))[0]
    squares = jnp.zeros((), jnp.float32)
    for grad in grads:
        squares = squares + jnp.sum(grad * grad)
    grad_norm = jnp.sqrt(squares)
    clip = CLIP_AT / jnp.maximum(grad_norm, CLIP_AT)
    steps_taken = step_count[0].astype(jnp.float32)
    firsts = (m_qkv, m_out, m_up, m_down, m_emb, m_vectors)
    seconds = (v_qkv, v_out, v_up, v_down, v_emb, v_vectors)
    new_w, new_m, new_v = ([], [], [])
    for index in range(6):
        rate = LR_VECTOR if index == 5 else LR_MATRIX
        decay = 0.0 if index == 5 else DECAY
        result = adamw(params[index], grads[index] * clip, firsts[index], seconds[index], rate, decay, steps_taken)
        new_w.append(result[0])
        new_m.append(result[1])
        new_v.append(result[2])
    return (loss, grad_norm, new_w[0], new_w[1], new_w[2], new_w[3], new_w[4], new_w[5], new_m[0], new_m[1], new_m[2], new_m[3], new_m[4], new_m[5], new_v[0], new_v[1], new_v[2], new_v[3], new_v[4], new_v[5])
```

```python
import math

import jax
import jax.numpy as jnp
from jax import lax
from jax.sharding import Mesh, PartitionSpec as P

HD = 64
HIGH = lax.Precision.HIGH
LR_MATRIX = 0.03
LR_VECTOR = 0.2
DECAY = 0.1
CLIP_AT = 0.02
EPS = 1e-05
SWAP = ((0, 1), (1, 0))
AXES = ("dh", "dl", "hh", "hl")


def dot(a, b, ca, cb):
    return lax.dot_general(
        a, b, (((ca,), (cb,)), ((), ())), precision=HIGH, preferred_element_type=jnp.float32
    )


def swap(values, axis):
    return lax.ppermute(values, axis, SWAP)


def head_sum(part):
    half = part.shape[0] // 2
    mine = part[:half] + swap(part[half:], "hl")
    mine = mine + swap(mine, "hh")
    return jnp.concatenate([mine, swap(mine, "hl")], axis=0)


def gather_rows(block):
    near = lax.all_gather(block, "dh", axis=0, tiled=True)
    return jnp.concatenate([near, swap(near, "dl")], axis=0)


def scatter_rows(grad):
    half = grad.shape[0] // 2
    near = grad[:half] + swap(grad[half:], "dl")
    return lax.psum_scatter(near, "dh", scatter_dimension=0, tiled=True)


def norm_stats(x):
    centre = x - jnp.mean(x, axis=-1, keepdims=True)
    rstd = lax.rsqrt(jnp.mean(centre * centre, axis=-1, keepdims=True) + EPS)
    return centre * rstd, rstd


def norm_back(dn, nh, rstd):
    return rstd * (
        dn - jnp.mean(dn, axis=-1, keepdims=True) - nh * jnp.mean(dn * nh, axis=-1, keepdims=True)
    )


def gelu(u):
    return 0.5 * u * (1.0 + jnp.tanh(0.7978845608 * (u + 0.044715 * u * u * u)))


def gelu_slope(u):
    t = jnp.tanh(0.7978845608 * (u + 0.044715 * u * u * u))
    return 0.5 * (1.0 + t) + 0.5 * u * (1.0 - t * t) * 0.7978845608 * (1.0 + 3.0 * 0.044715 * u * u)


def roll_half(x, c, axis=0):
    half = x.shape[axis] // 2
    a = lax.slice_in_dim(x, 0, half, axis=axis)
    b = lax.slice_in_dim(x, half, 2 * half, axis=axis)
    return jnp.where(
        c == 0, jnp.concatenate([a, b], axis=axis), jnp.concatenate([b, a], axis=axis)
    )


def halves(ctx, qry):
    hc, hq = ctx.shape[0] // 2, qry.shape[0] // 2
    return jnp.concatenate([ctx[:hc], qry[:hq], ctx[hc:], qry[hq:]], axis=0)


def ctx_of(x, hc, hq):
    return jnp.concatenate([x[:hc], x[hc + hq : 2 * hc + hq]], axis=0)


def qry_of(x, hc, hq):
    return jnp.concatenate([x[hc : hc + hq], x[2 * hc + hq :]], axis=0)


def neighbour_mask(neigh, live, context_rows, c):
    words = context_rows // 32
    col = jnp.bitwise_xor(neigh, c * (context_rows // 2))
    bit = jnp.left_shift(live, jnp.bitwise_and(col, 31))
    at = jnp.right_shift(col, 5)
    word = jnp.sum(
        jnp.where(at[:, None, :] == jnp.arange(words, dtype=jnp.int32)[None, :, None], bit[:, None, :], 0),
        axis=-1,
    )
    spread = jnp.broadcast_to(word[:, :, None], word.shape + (32,)).reshape(word.shape[0], context_rows)
    shift = jnp.bitwise_and(jnp.arange(context_rows, dtype=jnp.int32), 31)
    return jnp.bitwise_and(jnp.right_shift(spread, shift[None, :]), 1)


def softmax_rows(s):
    top = jnp.max(s, axis=-1, keepdims=True)
    e = jnp.exp(s - top)
    return e / jnp.sum(e, axis=-1, keepdims=True)


def heads_dot(a, b, ca, cb):
    return lax.dot_general(
        a, b, (((ca,), (cb,)), ((0,), (0,))), precision=HIGH, preferred_element_type=jnp.float32
    )


def split_heads(x):
    return jnp.transpose(x.reshape(x.shape[0], -1, HD), (1, 0, 2))


def merge_heads(x):
    return jnp.transpose(x, (1, 0, 2)).reshape(x.shape[1], -1)


def adamw(weight, grad, first, second, rate, decay, steps_taken):
    first_new = 0.9 * first + 0.1 * grad
    second_new = 0.999 * second + 0.001 * grad * grad
    first_hat = first_new / (1.0 - jnp.power(0.9, steps_taken))
    second_hat = second_new / (1.0 - jnp.power(0.999, steps_taken))
    weight_new = weight - rate * (first_hat / (jnp.sqrt(second_hat) + 1e-08) + decay * weight)
    return (weight_new, first_new, second_new)


def on_device(
    features,
    targets,
    neighbours,
    nbr_mask,
    flags,
    step_count,
    w_qkv,
    w_out,
    w_up,
    w_down,
    emb_weight,
    vectors,
    m_qkv,
    m_out,
    m_up,
    m_down,
    m_emb,
    m_vectors,
    v_qkv,
    v_out,
    v_up,
    v_down,
    v_emb,
    v_vectors,
):
    depth = w_qkv.shape[0]
    micros = features.shape[0]
    rows = features.shape[2]
    feats = features.shape[3]
    queries = neighbours.shape[2]
    context = rows - queries
    hc, hq = context // 2, queries // 2
    width = w_qkv.shape[2] // 3
    c = lax.axis_index("hl")
    scale = HD ** (-0.5)

    small = gather_rows(jnp.concatenate([emb_weight, vectors], axis=1))
    emb, vec = small[:, :feats], small[:, feats:].T
    wq, wo, wu, wd = [], [], [], []
    for l in range(depth):
        packed = gather_rows(jnp.concatenate([w_qkv[l], w_out[l]], axis=1))
        wq.append(packed[:, : 3 * width])
        wo.append(packed[:, 3 * width :])
        wu.append(gather_rows(w_up[l]))
        wd.append(gather_rows(w_down[l]))

    def gain(col):
        return vec[col][None, :]

    tables = []
    for m in range(micros):
        feat = features[m, 0]
        feat = halves(roll_half(feat[:context], c), roll_half(feat[context:], c))
        t_ctx = roll_half(targets[m, 0][:context], c)
        t_qry = roll_half(targets[m, 0][context:], c)
        t_in = halves(t_ctx[:, None], jnp.zeros((queries, 1), jnp.float32))
        neigh = roll_half(neighbours[m, 0], c)
        live = roll_half(nbr_mask[m, 0], c)
        flag = roll_half(flags[m, 0], c).astype(jnp.float32)
        mask = neighbour_mask(neigh, live, context, c)
        x = dot(feat, emb, 1, 1) + t_in * gain(2 * depth + 1)
        tables.append(dict(feat=feat, t_in=t_in, t_qry=t_qry, flag=flag, mask=mask, x=x))
    full_mask = [
        halves(jnp.ones((context, context), jnp.int32), t["mask"])[None] > 0 for t in tables
    ]
    qry_mask = [t["mask"][None] > 0 for t in tables]

    saved = [[None] * depth for _ in range(micros)]
    xs = [t["x"] for t in tables]
    for l in range(depth):
        last = l == depth - 1
        for m in range(micros):
            x = xs[m]
            nh, rstd = norm_stats(x)
            n = nh * gain(l)
            nq = qry_of(n, hc, hq) if last else n
            nc = ctx_of(n, hc, hq)
            q = split_heads(dot(nq, wq[l][:, :width], 1, 0))
            kv = dot(nc, wq[l][:, width:], 1, 0)
            k, v = split_heads(kv[:, :width]), split_heads(kv[:, width:])
            s = heads_dot(q, k, 2, 2) * scale
            s = jnp.where(qry_mask[m] if last else full_mask[m], s, -1e30)
            p = softmax_rows(s)
            o = merge_heads(heads_dot(p, v, 2, 1))
            total = head_sum(dot(o, wo[l], 1, 1))
            base = qry_of(x, hc, hq) if last else x
            x1 = base + total
            saved[m][l] = dict(nh=nh, rstd=rstd, nq=nq, nc=nc, q=q, k=k, v=v, p=p, o=o)
            xs[m] = x1
        for m in range(micros):
            x1 = xs[m]
            nh, rstd = norm_stats(x1)
            n = nh * gain(depth + l)
            u = dot(n, wu[l], 1, 0)
            g = gelu(u)
            xs[m] = x1 + head_sum(dot(g, wd[l], 1, 1))
            saved[m][l].update(nh2=nh, rstd2=rstd, n2=n, u=u, g=g)

    grads = [dict() for _ in range(depth)]
    g_vec = [jnp.zeros((vec.shape[1],), jnp.float32) for _ in range(vec.shape[0])]

    def add(store, key, value):
        store[key] = value if key not in store else store[key] + value

    share = 1.0 / (lax.axis_size("hh") * lax.axis_size("hl"))
    loss_sum = jnp.zeros((), jnp.float32)
    dxs = []
    for m in range(micros):
        t = tables[m]
        nh, rstd = norm_stats(xs[m])
        nf = nh * gain(2 * depth)
        r = gain(2 * depth + 2)
        err = jnp.sum(nf * r, axis=1) - t["t_qry"]
        loss_sum = loss_sum + jnp.sum(t["flag"] * err * err)
        dpred = (2.0 * t["flag"] * err)[:, None]
        g_vec[2 * depth + 2] += share * jnp.sum(nf * dpred, axis=0)
        dy = dpred * r
        g_vec[2 * depth] += share * jnp.sum(dy * nh, axis=0)
        dxs.append(norm_back(dy * gain(2 * depth), nh, rstd))

    for l in reversed(range(depth)):
        last = l == depth - 1
        for m in range(micros):
            k_ = saved[m][l]
            dy = dxs[m]
            dg = dot(dy, wd[l], 1, 0)
            add(grads[l], "down", dot(dy, k_["g"], 0, 0))
            du = dg * gelu_slope(k_["u"])
            add(grads[l], "up", dot(k_["n2"], du, 0, 0))
            dn = head_sum(dot(du, wu[l], 1, 1))
            g_vec[depth + l] += share * jnp.sum(dn * k_["nh2"], axis=0)
            dxs[m] = dy + norm_back(dn * gain(depth + l), k_["nh2"], k_["rstd2"])
        for m in range(micros):
            k_ = saved[m][l]
            dy = dxs[m]
            q, k, v, p, o = k_["q"], k_["k"], k_["v"], k_["p"], k_["o"]
            do = dot(dy, wo[l], 1, 0)
            add(grads[l], "out", dot(dy, o, 0, 0))
            doh = split_heads(do)
            dp = heads_dot(doh, v, 2, 2)
            rowsum = jnp.sum(split_heads(do * o), axis=-1, keepdims=True)
            ds = p * (dp - rowsum) * scale
            dv = merge_heads(heads_dot(p, doh, 1, 1))
            dq = merge_heads(heads_dot(ds, k, 2, 1))
            dk = merge_heads(heads_dot(ds, q, 1, 1))
            dkv = jnp.concatenate([dk, dv], axis=1)
            add(
                grads[l],
                "qkv",
                jnp.concatenate([dot(k_["nq"], dq, 0, 0), dot(k_["nc"], dkv, 0, 0)], axis=1),
            )
            dn_q = dot(dq, wq[l][:, :width], 1, 1)
            dn_c = dot(dkv, wq[l][:, width:], 1, 1)
            if last:
                dn = halves(dn_c, dn_q)
                dres = halves(jnp.zeros((context, dy.shape[1]), jnp.float32), dy)
            else:
                dn = dn_q + halves(dn_c, jnp.zeros((queries, dy.shape[1]), jnp.float32))
                dres = dy
            if l > 0:
                dn = head_sum(dn)
                g_vec[l] += share * jnp.sum(dn * k_["nh"], axis=0)
                dxs[m] = dres + norm_back(dn * gain(l), k_["nh"], k_["rstd"])
            else:
                g_vec[l] += jnp.sum(dn * k_["nh"], axis=0)
                dxs[m] = share * dres + norm_back(dn * gain(l), k_["nh"], k_["rstd"])
    g_emb = 0.0
    for m in range(micros):
        t = tables[m]
        g_emb = g_emb + dot(dxs[m], t["feat"], 0, 0)
        g_vec[2 * depth + 1] += jnp.sum(dxs[m] * t["t_in"], axis=0)

    own_small = scatter_rows(jnp.concatenate([g_emb, jnp.stack(g_vec, axis=1)], axis=1))
    own_small = own_small + swap(own_small, "hl")
    own_small = own_small + swap(own_small, "hh")
    own = [[], [], [], []]
    for l in range(depth):
        packed = scatter_rows(jnp.concatenate([grads[l]["qkv"], grads[l]["out"]], axis=1))
        own[0].append(packed[:, : 3 * width])
        own[1].append(packed[:, 3 * width :])
        own[2].append(scatter_rows(grads[l]["up"]))
        own[3].append(scatter_rows(grads[l]["down"]))
    owned = [jnp.stack(o) for o in own] + [own_small[:, :feats], own_small[:, feats:]]

    squares = share * jnp.sum(own_small * own_small)
    for o in owned[:4]:
        squares = squares + jnp.sum(o * o)
    counted = share * jnp.sum(flags.astype(jnp.float32))
    sums = lax.psum(jnp.stack([squares, share * loss_sum, counted]), AXES)
    counted = jnp.maximum(sums[2], 1.0)
    loss = sums[1] / counted
    grad_norm = jnp.sqrt(sums[0]) / counted
    factor = CLIP_AT / jnp.maximum(grad_norm, CLIP_AT) / counted
    steps_taken = step_count[0].astype(jnp.float32)
    weights = (w_qkv, w_out, w_up, w_down, emb_weight, vectors)
    firsts = (m_qkv, m_out, m_up, m_down, m_emb, m_vectors)
    seconds = (v_qkv, v_out, v_up, v_down, v_emb, v_vectors)
    new_w, new_m, new_v = [], [], []
    for i in range(6):
        rate = LR_VECTOR if i == 5 else LR_MATRIX
        decay = 0.0 if i == 5 else DECAY
        result = adamw(weights[i], owned[i] * factor, firsts[i], seconds[i], rate, decay, steps_taken)
        new_w.append(result[0])
        new_m.append(result[1])
        new_v.append(result[2])
    return (loss, grad_norm, *new_w, *new_m, *new_v)


def solution(mesh):
    dp, head = mesh.shape["dp"], mesh.shape["head"]
    fine = Mesh(mesh.devices.reshape(dp // 2, 2, head // 2, 2), AXES)
    rows, cols = ("dh", "dl"), ("hh", "hl")
    data = (
        P(None, rows, None, None),
        P(None, rows, None),
        P(None, rows, None, None),
        P(None, rows, None, None),
        P(None, rows, None),
        P(),
    )
    params = (P(None, rows, cols),) * 4 + (P(rows, None),) * 2
    return jax.shard_map(
        on_device,
        mesh=fine,
        in_specs=data + params * 3,
        out_specs=(P(), P()) + params * 3,
        check_vma=False,
    )
```

```python
import functools

import jax
import jax.numpy as jnp
from jax import lax
from jax.experimental import pallas as pl
from jax.experimental.pallas import tpu as pltpu
from jax.sharding import Mesh, PartitionSpec as P

HD = 64
LR_MATRIX = 0.03
LR_VECTOR = 0.2
DECAY = 0.1
CLIP_AT = 0.02
EPS = 1e-05
SWAP = ((0, 1), (1, 0))
AXES = ("dh", "dl", "hh", "hl")
F32, BF16 = jnp.float32, jnp.bfloat16
ANY = pl.BlockSpec(memory_space=pl.ANY)
SMEM = pl.BlockSpec(memory_space=pltpu.SMEM)
VMEM = pl.BlockSpec(memory_space=pltpu.VMEM)
QSCALE = HD ** (-0.5)
COST = 20


def swap(values, axis):
    return lax.ppermute(values, axis, SWAP)


def head_sum(mine, theirs, before=None):
    first, second = (swap(t, "hl") for t in theirs)
    a = mine + jnp.concatenate([after(first, before), second], axis=0)
    c = swap(a, "hl")
    b = swap(a, "hh")
    return a, b, c, swap(b, "hl")


def gather_rows(block):
    near = lax.all_gather(block, "dh", axis=0, tiled=True)
    return near, swap(near, "dl")


def everyone_sum(values):
    values = jnp.broadcast_to(jnp.pad(values, (0, 128 - values.shape[0]))[None], (8, 128))
    for axis in ("hl", "hh", "dl"):
        values = values + swap(values, axis)
    size = lax.axis_size("dh")
    if size & (size - 1):
        return lax.psum(values, "dh")[0]
    step = 1
    while step < size:
        values = values + lax.ppermute(values, "dh", [(i, i ^ step) for i in range(size)])
        step *= 2
    return values[0]


def near_rows(near, far):
    return near + swap(far, "dl")


def scatter_near(near):
    return lax.psum_scatter(near, "dh", scatter_dimension=0, tiled=True)


def after(value, *others):
    others = [o for o in others if o is not None]
    return lax.optimization_barrier((value, *others))[0] if others else value


def split(a):
    hi = a.astype(BF16)
    return hi, (a - hi.astype(F32)).astype(BF16)


def dg(a, b, ca, cb):
    return lax.dot_general(a, b, (((ca,), (cb,)), ((), ())), preferred_element_type=F32)


def mm(a, b, ca, cb):
    return (dg(a[1], b[0], ca, cb) + dg(a[0], b[1], ca, cb)) + dg(a[0], b[0], ca, cb)


def norm_stats(x):
    centre = x - jnp.mean(x, axis=-1, keepdims=True)
    rstd = lax.rsqrt(jnp.mean(centre * centre, axis=-1, keepdims=True) + EPS)
    return centre * rstd, rstd


def norm_back(dn, nh, rstd):
    return rstd * (
        dn - jnp.mean(dn, axis=-1, keepdims=True) - nh * jnp.mean(dn * nh, axis=-1, keepdims=True)
    )


def gelu_parts(u):
    t = jnp.tanh(0.7978845608 * (u + 0.044715 * u * u * u))
    value = 0.5 * u * (1.0 + t)
    slope = 0.5 * (1.0 + t) + 0.5 * u * (1.0 - t * t) * 0.7978845608 * (1.0 + 3.0 * 0.044715 * u * u)
    return value, slope


def lanes(shape, low):
    at = lax.broadcasted_iota(jnp.int32, shape, 1)
    return (at >= low) & (at < low + HD)


def keep(pair, low):
    held = lanes(pair[0].shape, low)
    zero = jnp.zeros(pair[0].shape, BF16)
    return jnp.where(held, pair[0], zero), jnp.where(held, pair[1], zero)


class Copies:
    def __init__(self, sems):
        self.sems, self.count, self.open = sems, 0, []

    def start(self, src, dst):
        copy = pltpu.make_async_copy(src, dst, self.sems.at[self.count])
        self.count += 1
        copy.start()
        self.open.append(copy)
        return copy

    def wait(self, *copies):
        for copy in copies:
            copy.wait()
            self.open = [other for other in self.open if other is not copy]

    def wait_all(self):
        self.wait(*list(self.open))


def load_pair(copies, near, far, dst):
    half = near.shape[0]
    return (
        copies.start(near, dst.at[pl.ds(0, half)]),
        copies.start(far, dst.at[pl.ds(half, half)]),
    )


def send_parts(copies, part, half, mine, theirs):
    quarter = half // 2
    for i, piece in enumerate(theirs):
        copies.start(part.at[pl.ds(half + i * quarter, quarter)], piece)
    if mine is not None:
        copies.start(part.at[pl.ds(0, half)], mine)


def row(vec_ref, index):
    return vec_ref[pl.ds(index, 1), :]


def run(kernel, name, inputs, specs, outs, scratch, sems, flops, moved, aliases=None):
    return pl.pallas_call(
        kernel,
        name=name,
        out_shape=[jax.ShapeDtypeStruct(s, F32) for s in outs],
        in_specs=specs,
        out_specs=[ANY] * len(outs),
        scratch_shapes=list(scratch) + [pltpu.SemaphoreType.DMA((sems,))],
        input_output_aliases=aliases or {},
        compiler_params=pltpu.CompilerParams(vmem_limit_bytes=56 << 20),
        cost_estimate=pl.CostEstimate(flops=flops // COST, bytes_accessed=moved // COST, transcendentals=0),
    )(*inputs)


class Sizes:
    def __init__(self, d, context, queries, depth, width, feats, share):
        self.d, self.context, self.queries = d, context, queries
        self.depth, self.width, self.feats, self.share = depth, width, feats, share
        self.hc, self.hq = context // 2, queries // 2
        self.half = self.hc + self.hq
        self.rows = context + queries
        self.heads = width // HD
        self.k = slice(0, 256)
        self.v = slice(128, 384)
        self.q = slice(384, 640)
        self.o = slice(512, 768)
        self.kv = slice(0, 384)


def load_feats(copies, z, c_ref, feat, dst):
    c = c_ref[0]
    made = []
    for i in range(2):
        side = c if i == 0 else 1 - c
        made.append(
            copies.start(
                feat.at[pl.ds(pl.multiple_of(side * z.hc, z.hc), z.hc)],
                dst.at[pl.ds(i * z.half, z.hc)],
            )
        )
        made.append(
            copies.start(
                feat.at[pl.ds(pl.multiple_of(z.context + side * z.hq, z.hq), z.hq)],
                dst.at[pl.ds(i * z.half + z.hc, z.hq)],
            )
        )
    return made


def split_into(hi, lo, value):
    a, b = split(value)
    hi[...] = a
    lo[...] = b


def scores(z, qh, kh, h, mask, masked_from):
    s = mm(keep(qh, h * HD), kh, 1, 1)
    if masked_from == 0:
        return jnp.where(mask > 0, s, -1e30)
    low = jnp.where(mask > 0, s[masked_from:], -1e30)
    return jnp.concatenate([s[:masked_from], low], axis=0)


def attn_fwd_kernel(z, l, first, last, *refs):
    if first:
        (c_ref, t_in, vec, feat, emb, wn, wf, mask) = refs[:8]
        refs = refs[8:]
    else:
        (vec, xp, pa, pb, pc, pd, wn, wf, mask) = refs[:9]
        refs = refs[9:]
    x_out, q_out, kv_out, o_out, lse_out, mine, *theirs = refs[:8]
    (xb, wb, wh, wl, qb, kvb, ob, lseb, part, maskb, *rest, sems) = refs[8:]
    copies = Copies(sems)
    if first:
        featb, embb = rest
        cf = load_feats(copies, z, c_ref, feat, featb)
        ce = copies.start(emb, embb)
    else:
        (add,) = rest
        cx = copies.start(xp, xb)
        ca = [
            copies.start(p, add.at[pl.ds(i * z.half, z.half)]) for i, p in enumerate((pa, pb, pc, pd))
        ]
    cw = load_pair(copies, wn, wf, wb)
    cm = copies.start(mask, maskb)
    if first:
        copies.wait(*cf, ce)
        embs = split(embb[...])
    else:
        copies.wait(cx, *ca)
    gain = row(vec, l)
    normed = []
    outs = []
    for i in range(2):
        here = pl.ds(i * z.half, z.half)
        if first:
            x = mm(split(featb[here, :]), embs, 1, 1) + t_in[here, :] * row(vec, 2 * z.depth + 1)
        else:
            x = xb[here, :] + (
                add[pl.ds(2 * i * z.half, z.half), :] + add[pl.ds((2 * i + 1) * z.half, z.half), :]
            )
        xb[here, :] = x
        outs.append(copies.start(xb.at[here], x_out.at[here]))
    copies.wait(*cw)
    split_into(wh, wl, wb[...])
    for i in range(2):
        here = pl.ds(i * z.half, z.half)
        nh, _ = norm_stats(xb[here, :])
        n = split(nh * gain)
        nc = (n[0][: z.hc], n[1][: z.hc])
        nq = (n[0][z.hc :], n[1][z.hc :]) if last else n
        qrows = pl.ds(i * z.hq, z.hq) if last else here
        qb[qrows, :] = mm(nq, (wh[:, z.q], wl[:, z.q]), 1, 0) * QSCALE
        kvb[pl.ds(i * z.hc, z.hc), :] = mm(nc, (wh[:, z.kv], wl[:, z.kv]), 1, 0)
    copies.start(qb, q_out)
    copies.start(kvb, kv_out)
    copies.wait(cm)
    kh = split(kvb[:, z.k])
    vh = split(kvb[:, z.v])
    vm = [keep(vh, HD + h * HD) for h in range(z.heads)]
    tiles = [(0, 2 * z.hq)] if last else [(z.half, z.half), (0, z.half)]
    for start, size in tiles:
        here = pl.ds(start, size)
        qh = split(qb[here, :])
        m_tile = maskb[...] if last else maskb[pl.ds((start // z.half) * z.hq, z.hq), :]
        o = jnp.zeros((size, 256), F32)
        lse = jnp.zeros((size, 128), F32)
        at = lax.broadcasted_iota(jnp.int32, (size, 128), 1)
        for h in range(z.heads):
            s = scores(z, qh, kh, h, m_tile, 0 if last else z.hc)
            top = jnp.max(s, axis=-1, keepdims=True)
            e = jnp.exp(s - top)
            total = jnp.sum(e, axis=-1, keepdims=True)
            o = o + mm(split(e), vm[h], 1, 0) * (1.0 / total)
            lse = jnp.where(at == h, top + jnp.log(total), lse)
        ob[here, :] = o
        lseb[here, :] = lse
        part[here, :] = mm(split(o), (wh[:, z.o], wl[:, z.o]), 1, 1)
        if start > 0:
            send_parts(copies, part, z.half, None, theirs)
    if last:
        send_parts(copies, part, z.hq, mine, theirs)
    else:
        copies.start(part.at[pl.ds(0, z.half)], mine)
    copies.start(ob, o_out)
    copies.start(lseb, lse_out)
    copies.wait_all()


def attn_fwd(z, l, last, inputs):
    first = l == 0
    rq = z.queries if last else z.rows
    scratch = [
        pltpu.VMEM((z.rows, z.d), F32),
        pltpu.VMEM((z.d, z.d), F32),
        pltpu.VMEM((z.d, z.d), BF16),
        pltpu.VMEM((z.d, z.d), BF16),
        pltpu.VMEM((rq, 256), F32),
        pltpu.VMEM((z.context, 384), F32),
        pltpu.VMEM((rq, 256), F32),
        pltpu.VMEM((rq, 128), F32),
        pltpu.VMEM((rq, z.d), F32),
        pltpu.VMEM((z.queries, z.context), F32),
    ]
    if first:
        scratch += [pltpu.VMEM((z.rows, z.feats), F32), pltpu.VMEM((z.d, z.feats), F32)]
        specs = [SMEM, VMEM, VMEM] + [ANY] * 5
    else:
        scratch += [pltpu.VMEM((4 * z.half, z.d), F32)]
        specs = [VMEM] + [ANY] * 8
    outs = [
        (z.rows, z.d),
        (rq, 256),
        (z.context, 384),
        (rq, 256),
        (rq, 128),
        (rq // 2, z.d),
        (rq // 4, z.d),
        (rq // 4, z.d),
    ]
    return run(
        functools.partial(attn_fwd_kernel, z, l, first, last),
        f"attn_fwd{l}",
        inputs,
        specs,
        outs,
        scratch,
        24,
        3 * 2 * (2 * rq * z.d * 256 + z.context * z.d * 384 + 6 * rq * z.context * 256),
        16 << 20,
    )


def ffn_fwd_kernel(z, l, last, *refs):
    (vec, xp, pa, pb, pc, pd, un, uf, dn, df) = refs[:10]
    x_out, u_out, mine, *theirs = refs[10:15]
    (xb, add, wb, wh, wl, vb, vh, vl, ub, part, sems) = refs[15:]
    copies = Copies(sems)
    half = z.hq if last else z.half
    if last:
        cx = [
            copies.start(xp.at[pl.ds(z.hc, z.hq)], xb.at[pl.ds(0, z.hq)]),
            copies.start(xp.at[pl.ds(z.half + z.hc, z.hq)], xb.at[pl.ds(z.hq, z.hq)]),
        ]
    else:
        cx = [copies.start(xp, xb)]
    ca = [copies.start(p, add.at[pl.ds(i * half, half)]) for i, p in enumerate((pa, pb, pc, pd))]
    cu = load_pair(copies, un, uf, wb)
    cd = load_pair(copies, dn, df, vb)
    copies.wait(*cx, *ca)
    gain = row(vec, z.depth + l)
    for i in range(2):
        here = pl.ds(i * half, half)
        xb[here, :] = xb[here, :] + (
            add[pl.ds(2 * i * half, half), :] + add[pl.ds((2 * i + 1) * half, half), :]
        )
    copies.start(xb, x_out)
    copies.wait(*cu)
    split_into(wh, wl, wb[...])
    copies.wait(*cd)
    split_into(vh, vl, vb[...])
    tiles = [(0, 2 * half)] if last else [(half, half), (0, half)]
    for start, size in tiles:
        here = pl.ds(start, size)
        nh, _ = norm_stats(xb[here, :])
        u = mm(split(nh * gain), (wh[...], wl[...]), 1, 0)
        ub[here, :] = u
        copies.start(ub.at[here], u_out.at[here])
        g, _ = gelu_parts(u)
        part[here, :] = mm(split(g), (vh[...], vl[...]), 1, 1)
        if start > 0:
            send_parts(copies, part, half, None, theirs)
    if last:
        send_parts(copies, part, half, mine, theirs)
    else:
        copies.start(part.at[pl.ds(0, half)], mine)
    copies.wait_all()


def ffn_fwd(z, l, last, inputs):
    r = z.queries if last else z.rows
    big = lambda t=F32: pltpu.VMEM((z.d, z.d), t)
    tall = lambda: pltpu.VMEM((r, z.d), F32)
    return run(
        functools.partial(ffn_fwd_kernel, z, l, last),
        f"ffn_fwd{l}",
        inputs,
        [VMEM] + [ANY] * 9,
        [(r, z.d), (r, z.d), (r // 2, z.d), (r // 4, z.d), (r // 4, z.d)],
        [tall(), pltpu.VMEM((2 * r, z.d), F32), big(), big(BF16), big(BF16), big(), big(BF16), big(BF16), tall(), tall()],
        20,
        3 * 4 * r * z.d * z.d,
        24 << 20,
    )


def ffn_bwd_kernel(z, l, last, accumulate, *refs):
    if last:
        (vec, side, xm, pa, pb, pc, pd, u_in, un, uf, dn, df) = refs[:12]
        refs = refs[12:]
    else:
        (vec, res, xn, xm, pa, pb, pc, pd, u_in, un, uf, dn, df) = refs[:13]
        refs = refs[13:]
    if accumulate:
        olds, refs = refs[:4], refs[4:]
    dy_out, mine, *theirs, gv, gun, guf, gdn, gdf = refs[:9]
    (xb, add, wb, wh, wl, vb, vh, vl, ub, dyb, dyh, dyl, gh, gl, part, gub, gdb, gvb, *rest, sems) = refs[9:]
    copies = Copies(sems)
    r = z.queries if last else z.rows
    half = r // 2
    ca = [copies.start(p, add.at[pl.ds(i * half, half)]) for i, p in enumerate((pa, pb, pc, pd))]
    cx = [copies.start(xm, xb)]
    if not last:
        (xnb,) = rest
        ca.append(copies.start(xn, xnb))
        for i in range(2):
            ca.append(copies.start(res.at[pl.ds(i * z.hq, z.hq)], dyb.at[pl.ds(i * z.half + z.hc, z.hq)]))
    cd = load_pair(copies, dn, df, vb)
    cu_in = copies.start(u_in, ub)
    cu = load_pair(copies, un, uf, wb)
    if accumulate:
        co = (*load_pair(copies, olds[0], olds[1], gub), *load_pair(copies, olds[2], olds[3], gdb))
    gvb[...] = jnp.zeros_like(gvb)
    copies.wait(*ca, *cx)
    for i in range(2):
        here = pl.ds(i * half, half)
        total = add[pl.ds(2 * i * half, half), :] + add[pl.ds((2 * i + 1) * half, half), :]
        if last:
            x4 = xb[here, :] + total
            nh, rstd = norm_stats(x4)
            r_head = row(vec, 2 * z.depth + 2)
            gain = row(vec, 2 * z.depth)
            nf = nh * gain
            flag = side[here, 0:1]
            err = jnp.sum(nf * r_head, axis=-1, keepdims=True) - side[here, 1:2]
            dpred = 2.0 * flag * err
            dnf = dpred * r_head
            dy = norm_back(dnf * gain, nh, rstd)
            gvb[pl.ds(2 * z.depth + 2, 1), :] += z.share * jnp.sum(nf * dpred, axis=0, keepdims=True)
            gvb[pl.ds(2 * z.depth, 1), :] += z.share * jnp.sum(dnf * nh, axis=0, keepdims=True)
            gvb[pl.ds(7, 1), :] += jnp.broadcast_to(
                jnp.sum(flag * err * err, axis=0, keepdims=True), (1, z.d)
            )
        else:
            gain = row(vec, l + 1)
            nh, rstd = norm_stats(xnb[here, :])
            dy = norm_back(total * gain, nh, rstd)
            dy = jnp.concatenate([dy[: z.hc], dy[z.hc :] + dyb[pl.ds(i * z.half + z.hc, z.hq), :]], axis=0)
            gvb[pl.ds(l + 1, 1), :] += z.share * jnp.sum(total * nh, axis=0, keepdims=True)
        dyb[here, :] = dy
        a, b = split(dy)
        dyh[here, :] = a
        dyl[here, :] = b
    copies.start(dyb, dy_out)
    copies.start(gvb, gv)
    copies.wait(*cd)
    split_into(vh, vl, vb[...])
    copies.wait(*cu)
    split_into(wh, wl, wb[...])
    copies.wait(cu_in)
    gain = row(vec, z.depth + l)
    tiles = [(0, r)] if last else [(half, half), (0, half)]
    for start, size in tiles:
        here = pl.ds(start, size)
        dh = mm((dyh[here, :], dyl[here, :]), (vh[...], vl[...]), 1, 0)
        g, slope = gelu_parts(ub[here, :])
        a, b = split(g)
        gh[here, :] = a
        gl[here, :] = b
        ub[here, :] = dh * slope
        part[here, :] = mm(split(ub[here, :]), (wh[...], wl[...]), 1, 1)
        if start > 0:
            send_parts(copies, part, half, None, theirs)
    if last:
        send_parts(copies, part, half, mine, theirs)
    else:
        copies.start(part.at[pl.ds(0, half)], mine)
    if accumulate:
        copies.wait(*co)
    new = mm((dyh[...], dyl[...]), (gh[...], gl[...]), 0, 0)
    gdb[...] = gdb[...] + new if accumulate else new
    d_half = z.d // 2
    copies.start(gdb.at[pl.ds(0, d_half)], gdn)
    copies.start(gdb.at[pl.ds(d_half, d_half)], gdf)
    nh, _ = norm_stats(xb[...])
    new = mm(split(nh * gain), split(ub[...]), 0, 0)
    gub[...] = gub[...] + new if accumulate else new
    copies.start(gub.at[pl.ds(0, d_half)], gun)
    copies.start(gub.at[pl.ds(d_half, d_half)], guf)
    copies.wait_all()


def ffn_bwd(z, l, last, inputs, olds):
    r = z.queries if last else z.rows
    big = lambda t=F32: pltpu.VMEM((z.d, z.d), t)
    tall = lambda t=F32: pltpu.VMEM((r, z.d), t)
    scratch = [tall(), pltpu.VMEM((2 * r, z.d), F32), big(), big(BF16), big(BF16), big(), big(BF16), big(BF16)]
    scratch += [tall(), tall(), tall(BF16), tall(BF16), tall(BF16), tall(BF16), tall(), big(), big()]
    scratch += [pltpu.VMEM((8, z.d), F32)]
    specs = [VMEM] + ([VMEM] if last else [ANY]) + [ANY] * (len(inputs) - 2)
    if not last:
        scratch += [tall()]
    h = z.d // 2
    outs = [(r, z.d), (r // 2, z.d), (r // 4, z.d), (r // 4, z.d), (8, z.d)] + [(h, z.d)] * 4
    aliases = None
    if olds is not None:
        aliases = {len(inputs) + i: 5 + i for i in range(4)}
        inputs = list(inputs) + list(olds)
        specs = specs + [ANY] * 4
    return run(
        functools.partial(ffn_bwd_kernel, z, l, last, olds is not None),
        f"ffn_bwd{l}",
        inputs,
        specs,
        outs,
        scratch,
        36,
        3 * 8 * r * z.d * z.d,
        32 << 20,
        aliases,
    )


def attn_bwd_kernel(z, l, first, last, accumulate, *refs):
    (vec, dyp, xm, pa, pb, pc, pd, wn, wf, x_in, q_in, kv_in, o_in, lse_in, mask) = refs[:15]
    refs = refs[15:]
    if first:
        (c_ref, t_in, feat) = refs[:3]
        refs = refs[3:]
    if accumulate:
        olds, refs = refs[: 3 if first else 2], refs[3 if first else 2 :]
    if first:
        gv, gn, gf, emb_out = refs[:4]
        refs = refs[4:]
    else:
        dy_out, mine, *theirs, gv, gn, gf = refs[:7]
        refs = refs[7:]
    (dyb, xmb, add, wb, wh, wl, xb, qb, kvb, ob, lseb, maskb, dyh, dyl, dqb, dkb, dvb, gb, gvb, *rest, sems) = refs
    copies = Copies(sems)
    rq = z.queries if last else z.rows
    half = rq // 2
    ca = [copies.start(p, add.at[pl.ds(i * half, half)]) for i, p in enumerate((pa, pb, pc, pd))]
    ca += [copies.start(dyp, dyb), copies.start(xm, xmb)]
    cw = load_pair(copies, wn, wf, wb)
    cq = [copies.start(q_in, qb), copies.start(kv_in, kvb), copies.start(o_in, ob)]
    cq += [copies.start(lse_in, lseb), copies.start(mask, maskb)]
    cx = [copies.start(x_in, xb)]
    if first:
        featb, geb = rest
        cx += load_feats(copies, z, c_ref, feat, featb)
    if accumulate:
        co = list(load_pair(copies, olds[0], olds[1], gb))
        if first:
            co.append(copies.start(olds[2], geb))
    gvb[...] = jnp.zeros_like(gvb)
    copies.wait(*ca)
    gain2 = row(vec, z.depth + l)
    for i in range(2):
        here = pl.ds(i * half, half)
        total = add[pl.ds(2 * i * half, half), :] + add[pl.ds((2 * i + 1) * half, half), :]
        nh, rstd = norm_stats(xmb[here, :])
        dy = dyb[here, :] + norm_back(total * gain2, nh, rstd)
        gvb[pl.ds(z.depth + l, 1), :] += z.share * jnp.sum(total * nh, axis=0, keepdims=True)
        dyb[here, :] = dy
        a, b = split(dy)
        dyh[here, :] = a
        dyl[here, :] = b
    if not first:
        copies.start(dyb, dy_out)
    copies.wait(*cw)
    split_into(wh, wl, wb[...])
    copies.wait(*cq)
    kh = split(kvb[:, z.k])
    vh = split(kvb[:, z.v])
    km = [keep(kh, h * HD) for h in range(z.heads)]
    dkb[...] = jnp.zeros_like(dkb)
    dvb[...] = jnp.zeros_like(dvb)
    tiles = [(0, rq)] if last else [(half, half), (0, half)]
    for start, size in tiles:
        here = pl.ds(start, size)
        do = mm((dyh[here, :], dyl[here, :]), (wh[:, z.o], wl[:, z.o]), 1, 0)
        doh = split(do)
        prod = do * ob[here, :]
        qh = split(qb[here, :])
        m_tile = maskb[...] if last else maskb[pl.ds((start // half) * z.hq, z.hq), :]
        dq = jnp.zeros((size, 256), F32)
        for h in range(z.heads):
            qm = keep(qh, h * HD)
            dm = keep(doh, HD + h * HD)
            s = scores(z, qh, kh, h, m_tile, 0 if last else z.hc)
            p = jnp.exp(s - lseb[here, h : h + 1])
            delta = jnp.sum(
                jnp.where(lanes(prod.shape, HD + h * HD), prod, 0.0), axis=-1, keepdims=True
            )
            dp = mm(dm, vh, 1, 1)
            ds = split(p * (dp - delta))
            dq = dq + mm(ds, km[h], 1, 0)
            dkb[...] += mm(ds, qm, 0, 0)
            dvb[...] += mm(split(p), dm, 0, 0)
        dqb[here, :] = dq * QSCALE
    kvb[:, 0:128] = dkb[:, 0:128]
    kvb[:, 128:256] = dkb[:, 128:256] + dvb[:, 0:128]
    kvb[:, 256:384] = dvb[:, 128:256]
    if accumulate:
        copies.wait(*co)
    g_out = mm((dyh[...], dyl[...]), split(ob[...]), 0, 0)
    copies.wait(*cx)
    gain = row(vec, l)
    dnb = add
    g_q = jnp.zeros((z.d, 256), F32)
    g_kv = jnp.zeros((z.d, 384), F32)
    ge = 0.0
    for i in (1, 0):
        here = pl.ds(i * z.half, z.half)
        nh, rstd = norm_stats(xb[here, :])
        n = split(nh * gain)
        nc = (n[0][: z.hc], n[1][: z.hc])
        nq = (n[0][z.hc :], n[1][z.hc :]) if last else n
        qrows = pl.ds(i * z.hq, z.hq) if last else here
        dq = split(dqb[qrows, :])
        dkv = split(kvb[pl.ds(i * z.hc, z.hc), :])
        g_q = g_q + mm(nq, dq, 0, 0)
        g_kv = g_kv + mm(nc, dkv, 0, 0)
        dn_q = mm(dq, (wh[:, z.q], wl[:, z.q]), 1, 1)
        dn_c = mm(dkv, (wh[:, z.kv], wl[:, z.kv]), 1, 1)
        if last:
            dn = jnp.concatenate([dn_c, dn_q], axis=0)
        else:
            dn = jnp.concatenate([dn_q[: z.hc] + dn_c, dn_q[z.hc :]], axis=0)
        if first:
            gvb[pl.ds(l, 1), :] += jnp.sum(dn * nh, axis=0, keepdims=True)
            dx = z.share * dyb[here, :] + norm_back(dn * gain, nh, rstd)
            gvb[pl.ds(2 * z.depth + 1, 1), :] += jnp.sum(dx * t_in[here, :], axis=0, keepdims=True)
            ge = ge + mm(split(dx), split(featb[here, :]), 0, 0)
        else:
            dnb[pl.ds(i * z.half, z.half), :] = dn
            if i > 0:
                send_parts(copies, dnb, z.half, None, theirs)
            else:
                copies.start(dnb.at[here], mine)
    copies.start(gvb, gv)
    new = [
        g_kv,
        g_q[:, 0:128],
        g_q[:, 128:256] + g_out[:, 0:128],
        g_out[:, 128:256],
    ]
    at = 0
    for piece in new:
        cols = slice(at, at + piece.shape[1])
        gb[:, cols] = gb[:, cols] + piece if accumulate else piece
        at += piece.shape[1]
    d_half = z.d // 2
    copies.start(gb.at[pl.ds(0, d_half)], gn)
    copies.start(gb.at[pl.ds(d_half, d_half)], gf)
    if first:
        geb[...] = geb[...] + ge if accumulate else ge
        copies.start(geb, emb_out)
    copies.wait_all()


def attn_bwd(z, l, last, inputs, firsts, olds):
    first = l == 0
    rq = z.queries if last else z.rows
    big = lambda t=F32: pltpu.VMEM((z.d, z.d), t)
    tall = lambda t=F32: pltpu.VMEM((rq, z.d), t)
    scratch = [tall(), tall(), pltpu.VMEM((2 * z.rows, z.d), F32), big(), big(BF16), big(BF16)]
    scratch += [pltpu.VMEM((z.rows, z.d), F32), pltpu.VMEM((rq, 256), F32), pltpu.VMEM((z.context, 384), F32)]
    scratch += [pltpu.VMEM((rq, 256), F32), pltpu.VMEM((rq, 128), F32), pltpu.VMEM((z.queries, z.context), F32)]
    scratch += [tall(BF16), tall(BF16), pltpu.VMEM((rq, 256), F32)]
    scratch += [pltpu.VMEM((z.context, 256), F32), pltpu.VMEM((z.context, 256), F32), big(), pltpu.VMEM((8, z.d), F32)]
    specs = [VMEM] + [ANY] * 14
    h = z.d // 2
    outs = [(8, z.d), (h, z.d), (h, z.d)]
    inputs = list(inputs)
    if first:
        inputs += list(firsts)
        specs += [SMEM, VMEM, ANY]
        scratch += [pltpu.VMEM((z.rows, z.feats), F32), pltpu.VMEM((z.d, z.feats), F32)]
        outs += [(z.d, z.feats)]
        grads = [1, 2, 3]
    else:
        outs = [(rq, z.d), (z.half, z.d), (z.half // 2, z.d), (z.half // 2, z.d)] + outs
        grads = [5, 6]
    aliases = None
    if olds is not None:
        aliases = {len(inputs) + i: g for i, g in enumerate(grads)}
        inputs += list(olds)
        specs += [ANY] * len(olds)
    return run(
        functools.partial(attn_bwd_kernel, z, l, first, last, olds is not None),
        f"attn_bwd{l}",
        inputs,
        specs,
        outs,
        scratch,
        32,
        3 * 2 * (4 * rq * z.d * 256 + 2 * z.context * z.d * 384 + 15 * rq * z.context * 256),
        24 << 20,
        aliases,
    )


def roll_half(x, c):
    half = x.shape[0] // 2
    return jnp.where(c == 0, x, jnp.concatenate([x[half:], x[:half]], axis=0))


def interleave(ctx, qry):
    hc, hq = ctx.shape[0] // 2, qry.shape[0] // 2
    return jnp.concatenate([ctx[:hc], qry[:hq], ctx[hc:], qry[hq:]], axis=0)


def neighbour_mask(neigh, live, context_rows, c):
    words = context_rows // 32
    col = jnp.bitwise_xor(neigh, c * (context_rows // 2))
    bit = jnp.left_shift(live, jnp.bitwise_and(col, 31))
    at = jnp.right_shift(col, 5)
    index = jnp.arange(words, dtype=jnp.int32)[None, :, None]
    word = jnp.sum(jnp.where(at[:, None, :] == index, bit[:, None, :], 0), axis=-1)
    spread = jnp.broadcast_to(word[:, :, None], word.shape + (32,)).reshape(word.shape[0], context_rows)
    shift = jnp.bitwise_and(jnp.arange(context_rows, dtype=jnp.int32), 31)
    return jnp.bitwise_and(jnp.right_shift(spread, shift[None, :]), 1).astype(F32)


def adamw(weight, grad, first, second, rate, decay, steps_taken):
    first_new = 0.9 * first + 0.1 * grad
    second_new = 0.999 * second + 0.001 * grad * grad
    first_hat = first_new / (1.0 - jnp.power(0.9, steps_taken))
    second_hat = second_new / (1.0 - jnp.power(0.999, steps_taken))
    weight_new = weight - rate * (first_hat / (jnp.sqrt(second_hat) + 1e-08) + decay * weight)
    return (weight_new, first_new, second_new)


def on_device(
    features,
    targets,
    neighbours,
    nbr_mask,
    flags,
    step_count,
    w_qkv,
    w_out,
    w_up,
    w_down,
    emb_weight,
    vectors,
    m_qkv,
    m_out,
    m_up,
    m_down,
    m_emb,
    m_vectors,
    v_qkv,
    v_out,
    v_up,
    v_down,
    v_emb,
    v_vectors,
):
    depth, d_rows = w_qkv.shape[:2]
    micros, _, rows, feats = features.shape
    queries = neighbours.shape[2]
    context = rows - queries
    width = w_qkv.shape[2] // 3
    d = d_rows * lax.axis_size("dh") * lax.axis_size("dl")
    share = 1.0 / (lax.axis_size("hh") * lax.axis_size("hl"))
    z = Sizes(d, context, queries, depth, width, feats, share)
    c = lax.axis_index("hl")
    c_arr = jnp.full((1,), c, jnp.int32)

    near, far = gather_rows(jnp.concatenate([emb_weight, vectors], axis=1))
    small = jnp.concatenate([near, far], axis=0)
    emb = small[:, :feats]
    vec = jnp.pad(small[:, feats:].T, ((0, 1), (0, 0)))
    def rows_near(block):
        return lax.all_gather(block, "dh", axis=0, tiled=True)

    blocks = []
    for l in range(depth):
        parts = [w_qkv[l][:, width:], w_qkv[l][:, :width], w_out[l]]
        blocks += [jnp.concatenate(parts, axis=1), w_up[l], w_down[l]]

    tables = []
    for m in range(micros):
        t_ctx = roll_half(targets[m, 0][:context], c)
        t_qry = roll_half(targets[m, 0][context:], c)
        t_in = interleave(t_ctx, jnp.zeros((queries,), F32))[:, None]
        flag = roll_half(flags[m, 0], c).astype(F32)
        mask = neighbour_mask(roll_half(neighbours[m, 0], c), roll_half(nbr_mask[m, 0], c), context, c)
        tables.append(dict(feat=features[m, 0], t_in=t_in, side=jnp.stack([flag, t_qry], axis=1), mask=mask))

    held = [vec]

    def beside(kernel, *transfers, ahead=(), strict=False):
        gate = after(held[0], *ahead)
        moved = [t() for t in transfers]
        outs = list(kernel(gate))
        moved = [after(x, outs[0]) for x in moved]
        held[0] = after(vec, *moved)
        if strict:
            outs[-1] = after(outs[-1], *moved)
        return (outs, *moved)

    def sent(pieces):
        held[0] = after(held[0], pieces[0])
        came[0] = pieces[1]
        return pieces

    came = [None]
    near, far = [None] * len(blocks), [None] * len(blocks)

    def gather(i):
        return lambda: rows_near(blocks[i])

    def cross(i, part=None):
        if part is None:
            return lambda: swap(near[i], "dl")
        half = near[i].shape[0] // 2
        return lambda: swap(near[i][part * half : (part + 1) * half], "dl")

    def both(i):
        return near[i], far[i]

    saved = [[None] * depth for _ in range(micros)]
    state = [None] * micros

    def attn_forward(l, m, *transfers, ahead=(), strict=False):
        t, last = tables[m], l == depth - 1

        def call(gate):
            if l == 0:
                inputs = (c_arr, t["t_in"], gate, t["feat"], emb, *both(3 * l), t["mask"])
            else:
                inputs = (gate, *state[m], *both(3 * l), t["mask"])
            return attn_fwd(z, l, last, inputs)

        (x, q, kv, o, lse, mine, *theirs), *moved = beside(call, *transfers, ahead=ahead, strict=strict)
        saved[m][l] = dict(x=x, q=q, kv=kv, o=o, lse=lse)
        state[m] = (x, *sent(head_sum(mine, theirs, came[0])))
        return moved

    def ffn_forward(l, m, *transfers, ahead=()):
        def call(gate):
            return ffn_fwd(z, l, l == depth - 1, (gate, *state[m], *both(3 * l + 1), *both(3 * l + 2)))

        (x1, u, mine, *theirs), *moved = beside(call, *transfers, ahead=ahead)
        saved[m][l].update(x1=x1, u=u)
        state[m] = (x1, *sent(head_sum(mine, theirs, came[0])))
        return moved

    near[0] = rows_near(blocks[0])
    far[0] = swap(near[0], "dl")
    near[1] = rows_near(blocks[1])
    far[1], near[2] = attn_forward(0, 0, cross(1), gather(2), ahead=(near[1],))
    near[3] = rows_near(blocks[3])
    (far[2],) = attn_forward(0, 1, cross(2), strict=True)
    (near[4],) = ffn_forward(0, 0, gather(4))
    far[3], near[5] = ffn_forward(0, 1, cross(3), gather(5))
    far[4] = swap(near[4], "dl")
    (top,) = attn_forward(1, 0, cross(5, 0))
    (low,) = attn_forward(1, 1, cross(5, 1))
    far[5] = jnp.concatenate([top, low], axis=0)
    ffn_forward(1, 0)
    ffn_forward(1, 1)

    g_attn, g_ffn = [None] * depth, [None] * depth
    g_vecs = []
    cot = [None] * micros

    def ffn_backward(l, m, *transfers):
        k, last = saved[m][l], l == depth - 1

        def call(gate):
            weights = (k["u"], *both(3 * l + 1), *both(3 * l + 2))
            if last:
                inputs = (gate, tables[m]["side"], k["x1"], *state[m][1:], *weights)
            else:
                res, pieces = cot[m]
                inputs = (gate, res, saved[m][l + 1]["x"], k["x1"], *pieces, *weights)
            return ffn_bwd(z, l, last, inputs, g_ffn[l])

        (dy, mine, t0, t1, gv, *g_ffn[l]), *moved = beside(call, *transfers)
        g_vecs.append(gv)
        cot[m] = (dy, sent(head_sum(mine, (t0, t1), came[0])))
        return moved

    def attn_backward(l, m, *transfers):
        k, t, last = saved[m][l], tables[m], l == depth - 1

        def call(gate):
            dy, pieces = cot[m]
            inputs = (gate, dy, k["x1"], *pieces, *both(3 * l), k["x"], k["q"], k["kv"], k["o"], k["lse"], t["mask"])
            firsts = (c_arr, t["t_in"], t["feat"]) if l == 0 else ()
            return attn_bwd(z, l, last, inputs, firsts, g_attn[l])

        outs, *moved = beside(call, *transfers)
        if l == 0:
            gv, *g_attn[l] = outs
        else:
            dy, mine, t0, t1, gv, *g_attn[l] = outs
            cot[m] = (dy, sent(head_sum(mine, (t0, t1), came[0])))
        g_vecs.append(gv)
        return moved

    def cross_far(pair):
        return lambda: swap(pair[1], "dl")

    def reduce(part):
        return lambda: scatter_near(part)

    ffn_backward(1, 0)
    ffn_backward(1, 1)
    up1, down1 = g_ffn[1][:2], g_ffn[1][2:]
    attn_backward(1, 0)
    (got,) = attn_backward(1, 1, cross_far(up1))
    own_up1 = up1[0] + got
    packed1 = g_attn[1][:2]
    got, own_up1 = ffn_backward(0, 0, cross_far(down1), reduce(own_up1))
    own_down1 = down1[0] + got
    got, own_down1 = ffn_backward(0, 1, cross_far(packed1), reduce(own_down1))
    own_packed1 = packed1[0] + got
    up0, down0 = g_ffn[0][:2], g_ffn[0][2:]
    own_up0 = near_rows(*up0)
    held[0] = after(held[0], own_up0)
    got, own_up0, own_packed1 = attn_backward(0, 0, cross_far(down0), reduce(own_up0), reduce(own_packed1))
    own_down0 = down0[0] + got
    (own_down0,) = attn_backward(0, 1, reduce(own_down0))
    packed0 = g_attn[0][:2]
    own_packed0 = near_rows(packed0[0], after(packed0[1], own_down0))
    crossed = own_packed0
    own_packed0 = scatter_near(own_packed0)
    own = [[own_packed0, own_packed1], [own_up0, own_up1], [own_down0, own_down1]]

    owned = [
        jnp.stack([jnp.concatenate([o[:, 2 * width : 3 * width], o[:, : 2 * width]], axis=1) for o in own[0]]),
        jnp.stack([o[:, 3 * width :] for o in own[0]]),
        jnp.stack(own[1]),
        jnp.stack(own[2]),
    ]
    g_vec = sum(g_vecs[1:], g_vecs[0])
    n_vec = vectors.shape[1]
    loss_local = g_vec[n_vec, 0]
    g_small = jnp.concatenate([g_attn[0][2], g_vec[:n_vec].T], axis=1)
    own_small = scatter_near(near_rows(g_small[: d // 2], g_small[d // 2 :]))
    own_small = own_small + swap(own_small, "hl")
    own_small = own_small + swap(own_small, "hh")
    owned += [own_small[:, :feats], own_small[:, feats:]]

    squares = share * jnp.sum(own_small * own_small)
    for o in owned[:4]:
        squares = squares + jnp.sum(o * o)
    counted = share * jnp.sum(flags.astype(F32))
    sums = everyone_sum(jnp.stack([squares, share * loss_local, counted]))
    counted = jnp.maximum(sums[2], 1.0)
    loss = sums[1] / counted
    grad_norm = jnp.sqrt(sums[0]) / counted
    factor = CLIP_AT / jnp.maximum(grad_norm, CLIP_AT) / counted
    steps_taken = step_count[0].astype(F32)
    weights = (w_qkv, w_out, w_up, w_down, emb_weight, vectors)
    firsts = (m_qkv, m_out, m_up, m_down, m_emb, m_vectors)
    seconds = (v_qkv, v_out, v_up, v_down, v_emb, v_vectors)
    new_w, new_m, new_v = [], [], []
    for i in range(6):
        rate = LR_VECTOR if i == 5 else LR_MATRIX
        decay = 0.0 if i == 5 else DECAY
        result = adamw(weights[i], owned[i] * factor, firsts[i], seconds[i], rate, decay, steps_taken)
        new_w.append(result[0])
        new_m.append(result[1])
        new_v.append(result[2])
    return (loss, grad_norm, *new_w, *new_m, *new_v)


def solution(mesh):
    dp, head = mesh.shape["dp"], mesh.shape["head"]
    fine = Mesh(mesh.devices.reshape(dp // 2, 2, head // 2, 2), AXES)
    rows, cols = ("dh", "dl"), ("hh", "hl")
    data = (
        P(None, rows, None, None),
        P(None, rows, None),
        P(None, rows, None, None),
        P(None, rows, None, None),
        P(None, rows, None),
        P(),
    )
    params = (P(None, rows, cols),) * 4 + (P(rows, None),) * 2
    return jax.shard_map(
        on_device,
        mesh=fine,
        in_specs=data + params * 3,
        out_specs=(P(), P()) + params * 3,
        check_vma=False,
    )
```

```python
import functools

import jax
import jax.numpy as jnp
from jax import lax
from jax.experimental import pallas as pl
from jax.experimental.pallas import tpu as pltpu
from jax.sharding import Mesh, PartitionSpec as P

HD = 64
LR_MATRIX = 0.03
LR_VECTOR = 0.2
DECAY = 0.1
CLIP_AT = 0.02
EPS = 1e-05
SWAP = ((0, 1), (1, 0))
AXES = ("dh", "dl", "hh", "hl")
F32, BF16 = jnp.float32, jnp.bfloat16
ANY = pl.BlockSpec(memory_space=pl.ANY)
SMEM = pl.BlockSpec(memory_space=pltpu.SMEM)
VMEM = pl.BlockSpec(memory_space=pltpu.VMEM)
QSCALE = HD ** (-0.5)
COST = 20


def swap(values, axis):
    return lax.ppermute(values, axis, SWAP)


def head_sum(mine, theirs, before=None):
    if before is not None and before.shape[0] < mine.shape[0]:
        theirs, before = [after(t, before) for t in theirs], None
    first, second = (swap(t, "hl") for t in theirs)
    a = mine + jnp.concatenate([after(first, before), second], axis=0)
    return [a, swap(a, "hh"), swap(a, "hl")]


def gather_rows(block):
    near = lax.all_gather(block, "dh", axis=0, tiled=True)
    return near, swap(near, "dl")


def everyone_sum(values):
    values = jnp.broadcast_to(jnp.pad(values, (0, 128 - values.shape[0]))[None], (8, 128))
    for axis in ("hl", "hh", "dl"):
        values = values + swap(values, axis)
    size = lax.axis_size("dh")
    if size & (size - 1):
        return lax.psum(values, "dh")[0]
    step = 1
    while step < size:
        values = values + lax.ppermute(values, "dh", [(i, i ^ step) for i in range(size)])
        step *= 2
    return values[0]


def near_rows(near, far):
    return near + swap(far, "dl")


def scatter_near(near):
    return lax.psum_scatter(near, "dh", scatter_dimension=0, tiled=True)


def after(value, *others):
    others = [o for o in others if o is not None]
    return lax.optimization_barrier((value, *others))[0] if others else value


def split(a):
    hi = a.astype(BF16)
    return hi, (a - hi.astype(F32)).astype(BF16)


def dg(a, b, ca, cb):
    return lax.dot_general(a, b, (((ca,), (cb,)), ((), ())), preferred_element_type=F32)


def mm(a, b, ca, cb):
    return (dg(a[1], b[0], ca, cb) + dg(a[0], b[1], ca, cb)) + dg(a[0], b[0], ca, cb)


def norm_stats(x):
    centre = x - jnp.mean(x, axis=-1, keepdims=True)
    rstd = lax.rsqrt(jnp.mean(centre * centre, axis=-1, keepdims=True) + EPS)
    return centre * rstd, rstd


def norm_back(dn, nh, rstd):
    return rstd * (
        dn - jnp.mean(dn, axis=-1, keepdims=True) - nh * jnp.mean(dn * nh, axis=-1, keepdims=True)
    )


def gelu_parts(u):
    t = jnp.tanh(0.7978845608 * (u + 0.044715 * u * u * u))
    value = 0.5 * u * (1.0 + t)
    slope = 0.5 * (1.0 + t) + 0.5 * u * (1.0 - t * t) * 0.7978845608 * (1.0 + 3.0 * 0.044715 * u * u)
    return value, slope


def lanes(shape, low):
    at = lax.broadcasted_iota(jnp.int32, shape, 1)
    return (at >= low) & (at < low + HD)


def keep(pair, low):
    held = lanes(pair[0].shape, low)
    zero = jnp.zeros(pair[0].shape, BF16)
    return jnp.where(held, pair[0], zero), jnp.where(held, pair[1], zero)


class Copies:
    def __init__(self, sems):
        self.sems, self.count, self.open = sems, 0, []

    def start(self, src, dst):
        copy = pltpu.make_async_copy(src, dst, self.sems.at[self.count])
        self.count += 1
        copy.start()
        self.open.append(copy)
        return copy

    def wait(self, *copies):
        for copy in copies:
            copy.wait()
            self.open = [other for other in self.open if other is not copy]

    def wait_all(self):
        self.wait(*list(self.open))


def load_pair(copies, near, far, dst):
    half = near.shape[0]
    return (
        copies.start(near, dst.at[pl.ds(0, half)]),
        copies.start(far, dst.at[pl.ds(half, half)]),
    )


def send_parts(copies, part, half, mine, theirs):
    quarter = half // 2
    for i, piece in enumerate(theirs):
        copies.start(part.at[pl.ds(half + i * quarter, quarter)], piece)
    if mine is not None:
        copies.start(part.at[pl.ds(0, half)], mine)


def load_weight(copies, arrays, dst, z_ref=None):
    if len(arrays) == 2:
        return load_pair(copies, arrays[0], arrays[1], dst)
    rows = dst.shape[0] // 8
    made = []
    for i in range(8):
        if len(arrays) == 1:
            src = arrays[0].at[pl.ds(((i % 4) * 2 + i // 4) * rows, rows)]
            at = i * rows
        else:
            src = arrays[i]
            at = pl.multiple_of((i // 4 * 4 + jnp.bitwise_xor(z_ref[1], i % 4)) * rows, 8)
        made.append(copies.start(src, dst.at[pl.ds(at, rows)]))
    return tuple(made)


def row(vec_ref, index):
    return vec_ref[pl.ds(index, 1), :]


def run(kernel, name, inputs, specs, outs, scratch, sems, flops, moved, aliases=None):
    return pl.pallas_call(
        kernel,
        name=name,
        out_shape=[jax.ShapeDtypeStruct(s, F32) for s in outs],
        in_specs=specs,
        out_specs=[ANY] * len(outs),
        scratch_shapes=list(scratch) + [pltpu.SemaphoreType.DMA((sems,))],
        input_output_aliases=aliases or {},
        compiler_params=pltpu.CompilerParams(vmem_limit_bytes=56 << 20),
        cost_estimate=pl.CostEstimate(flops=flops // COST, bytes_accessed=moved // COST, transcendentals=0),
    )(*inputs)


class Sizes:
    def __init__(self, d, context, queries, depth, width, feats, share):
        self.d, self.context, self.queries = d, context, queries
        self.depth, self.width, self.feats, self.share = depth, width, feats, share
        self.hc, self.hq = context // 2, queries // 2
        self.half = self.hc + self.hq
        self.rows = context + queries
        self.heads = width // HD
        self.k = slice(0, 256)
        self.v = slice(128, 384)
        self.q = slice(384, 640)
        self.o = slice(512, 768)
        self.kv = slice(0, 384)


def load_feats(copies, z, c_ref, feat, dst):
    c = c_ref[0]
    made = []
    for i in range(2):
        side = c if i == 0 else 1 - c
        made.append(
            copies.start(
                feat.at[pl.ds(pl.multiple_of(side * z.hc, z.hc), z.hc)],
                dst.at[pl.ds(i * z.half, z.hc)],
            )
        )
        made.append(
            copies.start(
                feat.at[pl.ds(pl.multiple_of(z.context + side * z.hq, z.hq), z.hq)],
                dst.at[pl.ds(i * z.half + z.hc, z.hq)],
            )
        )
    return made


def split_into(hi, lo, value):
    a, b = split(value)
    hi[...] = a
    lo[...] = b


def scores(z, qh, kh, h, mask, masked_from):
    s = mm(keep(qh, h * HD), kh, 1, 1)
    if masked_from == 0:
        return jnp.where(mask > 0, s, -1e30)
    low = jnp.where(mask > 0, s[masked_from:], -1e30)
    return jnp.concatenate([s[:masked_from], low], axis=0)


def attn_fwd_kernel(z, l, first, last, blocks, *refs):
    c_ref = None
    if first:
        (c_ref, t_in, vec, feat, emb, *weights, mask) = refs[: 6 + blocks]
        refs = refs[6 + blocks :]
    else:
        (vec, xp, pa, pb, pc, pd, *weights, mask) = refs[:9]
        refs = refs[9:]
    x_out, q_out, kv_out, o_out, lse_out, mine, *theirs = refs[:8]
    (xb, wb, wh, wl, qb, kvb, ob, lseb, part, maskb, *rest, sems) = refs[8:]
    copies = Copies(sems)
    if first:
        featb, embb = rest
        cf = load_feats(copies, z, c_ref, feat, featb)
        ce = copies.start(emb, embb)
    else:
        (add,) = rest
        cx = copies.start(xp, xb)
        ca = [
            copies.start(p, add.at[pl.ds(i * z.half, z.half)]) for i, p in enumerate((pa, pb, pc, pd))
        ]
    cw = load_weight(copies, weights, wb, c_ref)
    cm = copies.start(mask, maskb)
    if first:
        copies.wait(*cf, ce)
        embs = split(embb[...])
    else:
        copies.wait(cx, *ca)
    gain = row(vec, l)
    normed = []
    outs = []
    for i in range(2):
        here = pl.ds(i * z.half, z.half)
        if first:
            x = mm(split(featb[here, :]), embs, 1, 1) + t_in[here, :] * row(vec, 2 * z.depth + 1)
        else:
            x = xb[here, :] + (
                add[pl.ds(2 * i * z.half, z.half), :] + add[pl.ds((2 * i + 1) * z.half, z.half), :]
            )
        xb[here, :] = x
        outs.append(copies.start(xb.at[here], x_out.at[here]))
    copies.wait(*cw)
    split_into(wh, wl, wb[...])
    for i in range(2):
        here = pl.ds(i * z.half, z.half)
        nh, _ = norm_stats(xb[here, :])
        n = split(nh * gain)
        nc = (n[0][: z.hc], n[1][: z.hc])
        nq = (n[0][z.hc :], n[1][z.hc :]) if last else n
        qrows = pl.ds(i * z.hq, z.hq) if last else here
        qb[qrows, :] = mm(nq, (wh[:, z.q], wl[:, z.q]), 1, 0) * QSCALE
        kvb[pl.ds(i * z.hc, z.hc), :] = mm(nc, (wh[:, z.kv], wl[:, z.kv]), 1, 0)
    copies.start(qb, q_out)
    copies.start(kvb, kv_out)
    copies.wait(cm)
    kh = split(kvb[:, z.k])
    vh = split(kvb[:, z.v])
    vm = [keep(vh, HD + h * HD) for h in range(z.heads)]
    tiles = [(0, 2 * z.hq)] if last else [(z.half, z.half), (0, z.half)]
    for start, size in tiles:
        here = pl.ds(start, size)
        qh = split(qb[here, :])
        m_tile = maskb[...] if last else maskb[pl.ds((start // z.half) * z.hq, z.hq), :]
        o = jnp.zeros((size, 256), F32)
        lse = jnp.zeros((size, 128), F32)
        at = lax.broadcasted_iota(jnp.int32, (size, 128), 1)
        for h in range(z.heads):
            s = scores(z, qh, kh, h, m_tile, 0 if last else z.hc)
            top = jnp.max(s, axis=-1, keepdims=True)
            e = jnp.exp(s - top)
            total = jnp.sum(e, axis=-1, keepdims=True)
            o = o + mm(split(e), vm[h], 1, 0) * (1.0 / total)
            lse = jnp.where(at == h, top + jnp.log(total), lse)
        ob[here, :] = o
        lseb[here, :] = lse
        part[here, :] = mm(split(o), (wh[:, z.o], wl[:, z.o]), 1, 1)
        if start > 0:
            send_parts(copies, part, z.half, None, theirs)
    if last:
        send_parts(copies, part, z.hq, mine, theirs)
    else:
        copies.start(part.at[pl.ds(0, z.half)], mine)
    copies.start(ob, o_out)
    copies.start(lseb, lse_out)
    copies.wait_all()


def attn_fwd(z, l, last, blocks, inputs):
    first = l == 0
    rq = z.queries if last else z.rows
    scratch = [
        pltpu.VMEM((z.rows, z.d), F32),
        pltpu.VMEM((z.d, z.d), F32),
        pltpu.VMEM((z.d, z.d), BF16),
        pltpu.VMEM((z.d, z.d), BF16),
        pltpu.VMEM((rq, 256), F32),
        pltpu.VMEM((z.context, 384), F32),
        pltpu.VMEM((rq, 256), F32),
        pltpu.VMEM((rq, 128), F32),
        pltpu.VMEM((rq, z.d), F32),
        pltpu.VMEM((z.queries, z.context), F32),
    ]
    if first:
        scratch += [pltpu.VMEM((z.rows, z.feats), F32), pltpu.VMEM((z.d, z.feats), F32)]
        specs = [SMEM, VMEM, VMEM] + [ANY] * (3 + blocks)
    else:
        scratch += [pltpu.VMEM((4 * z.half, z.d), F32)]
        specs = [VMEM] + [ANY] * 8
    outs = [
        (z.rows, z.d),
        (rq, 256),
        (z.context, 384),
        (rq, 256),
        (rq, 128),
        (rq // 2, z.d),
        (rq // 4, z.d),
        (rq // 4, z.d),
    ]
    return run(
        functools.partial(attn_fwd_kernel, z, l, first, last, blocks),
        f"attn_fwd{l}",
        inputs,
        specs,
        outs,
        scratch,
        48,
        3 * 2 * (2 * rq * z.d * 256 + z.context * z.d * 384 + 6 * rq * z.context * 256),
        16 << 20,
    )


def ffn_fwd_kernel(z, l, last, blocks, *refs):
    (vec, xp, pa, pb, pc, pd, *weights) = refs[: 6 + sum(blocks)]
    refs = refs[6 + sum(blocks) :]
    ups, downs = weights[: blocks[0]], weights[blocks[0] :]
    x_out, u_out, mine, *theirs = refs[:5]
    (xb, add, wb, wh, wl, vb, vh, vl, ub, part, sems) = refs[5:]
    copies = Copies(sems)
    half = z.hq if last else z.half
    if last:
        cx = [
            copies.start(xp.at[pl.ds(z.hc, z.hq)], xb.at[pl.ds(0, z.hq)]),
            copies.start(xp.at[pl.ds(z.half + z.hc, z.hq)], xb.at[pl.ds(z.hq, z.hq)]),
        ]
    else:
        cx = [copies.start(xp, xb)]
    ca = [copies.start(p, add.at[pl.ds(i * half, half)]) for i, p in enumerate((pa, pb, pc, pd))]
    cu = load_weight(copies, ups, wb)
    cd = load_weight(copies, downs, vb)
    copies.wait(*cx, *ca)
    gain = row(vec, z.depth + l)
    for i in range(2):
        here = pl.ds(i * half, half)
        xb[here, :] = xb[here, :] + (
            add[pl.ds(2 * i * half, half), :] + add[pl.ds((2 * i + 1) * half, half), :]
        )
    copies.start(xb, x_out)
    copies.wait(*cu)
    split_into(wh, wl, wb[...])
    copies.wait(*cd)
    split_into(vh, vl, vb[...])
    tiles = [(0, 2 * half)] if last else [(half, half), (0, half)]
    for start, size in tiles:
        here = pl.ds(start, size)
        nh, _ = norm_stats(xb[here, :])
        u = mm(split(nh * gain), (wh[...], wl[...]), 1, 0)
        ub[here, :] = u
        copies.start(ub.at[here], u_out.at[here])
        g, _ = gelu_parts(u)
        part[here, :] = mm(split(g), (vh[...], vl[...]), 1, 1)
        if start > 0:
            send_parts(copies, part, half, None, theirs)
    if last:
        send_parts(copies, part, half, mine, theirs)
    else:
        copies.start(part.at[pl.ds(0, half)], mine)
    copies.wait_all()


def ffn_fwd(z, l, last, blocks, inputs):
    r = z.queries if last else z.rows
    big = lambda t=F32: pltpu.VMEM((z.d, z.d), t)
    tall = lambda: pltpu.VMEM((r, z.d), F32)
    return run(
        functools.partial(ffn_fwd_kernel, z, l, last, blocks),
        f"ffn_fwd{l}",
        inputs,
        [VMEM] + [ANY] * (5 + sum(blocks)),
        [(r, z.d), (r, z.d), (r // 2, z.d), (r // 4, z.d), (r // 4, z.d)],
        [tall(), pltpu.VMEM((2 * r, z.d), F32), big(), big(BF16), big(BF16), big(), big(BF16), big(BF16), tall(), tall()],
        48,
        3 * 4 * r * z.d * z.d,
        24 << 20,
    )


def ffn_bwd_kernel(z, l, last, accumulate, blocks, *refs):
    held = sum(blocks)
    if last:
        (vec, side, xm, pa, pb, pc, pd, u_in, *weights) = refs[: 8 + held]
        refs = refs[8 + held :]
    else:
        (vec, res, xn, xm, pa, pb, pc, pd, u_in, *weights) = refs[: 9 + held]
        refs = refs[9 + held :]
    ups, downs = weights[: blocks[0]], weights[blocks[0] :]
    if accumulate:
        olds, refs = refs[:4], refs[4:]
    dy_out, mine, *theirs, gv, gun, guf, gdn, gdf = refs[:9]
    (xb, add, wb, wh, wl, vb, vh, vl, ub, dyb, dyh, dyl, gh, gl, part, gub, gdb, gvb, *rest, sems) = refs[9:]
    copies = Copies(sems)
    r = z.queries if last else z.rows
    half = r // 2
    ca = [copies.start(p, add.at[pl.ds(i * half, half)]) for i, p in enumerate((pa, pb, pc, pd))]
    cx = [copies.start(xm, xb)]
    if not last:
        (xnb,) = rest
        ca.append(copies.start(xn, xnb))
        for i in range(2):
            ca.append(copies.start(res.at[pl.ds(i * z.hq, z.hq)], dyb.at[pl.ds(i * z.half + z.hc, z.hq)]))
    cd = load_weight(copies, downs, vb)
    cu_in = copies.start(u_in, ub)
    cu = load_weight(copies, ups, wb)
    if accumulate:
        co = (*load_pair(copies, olds[0], olds[1], gub), *load_pair(copies, olds[2], olds[3], gdb))
    gvb[...] = jnp.zeros_like(gvb)
    copies.wait(*ca, *cx)
    for i in range(2):
        here = pl.ds(i * half, half)
        total = add[pl.ds(2 * i * half, half), :] + add[pl.ds((2 * i + 1) * half, half), :]
        if last:
            x4 = xb[here, :] + total
            nh, rstd = norm_stats(x4)
            r_head = row(vec, 2 * z.depth + 2)
            gain = row(vec, 2 * z.depth)
            nf = nh * gain
            flag = side[here, 0:1]
            err = jnp.sum(nf * r_head, axis=-1, keepdims=True) - side[here, 1:2]
            dpred = 2.0 * flag * err
            dnf = dpred * r_head
            dy = norm_back(dnf * gain, nh, rstd)
            gvb[pl.ds(2 * z.depth + 2, 1), :] += z.share * jnp.sum(nf * dpred, axis=0, keepdims=True)
            gvb[pl.ds(2 * z.depth, 1), :] += z.share * jnp.sum(dnf * nh, axis=0, keepdims=True)
            gvb[pl.ds(7, 1), :] += jnp.broadcast_to(
                jnp.sum(flag * err * err, axis=0, keepdims=True), (1, z.d)
            )
        else:
            gain = row(vec, l + 1)
            nh, rstd = norm_stats(xnb[here, :])
            dy = norm_back(total * gain, nh, rstd)
            dy = jnp.concatenate([dy[: z.hc], dy[z.hc :] + dyb[pl.ds(i * z.half + z.hc, z.hq), :]], axis=0)
            gvb[pl.ds(l + 1, 1), :] += z.share * jnp.sum(total * nh, axis=0, keepdims=True)
        dyb[here, :] = dy
        a, b = split(dy)
        dyh[here, :] = a
        dyl[here, :] = b
    copies.start(dyb, dy_out)
    copies.start(gvb, gv)
    copies.wait(*cd)
    split_into(vh, vl, vb[...])
    copies.wait(*cu)
    split_into(wh, wl, wb[...])
    copies.wait(cu_in)
    gain = row(vec, z.depth + l)
    tiles = [(0, r)] if last else [(half, half), (0, half)]
    for start, size in tiles:
        here = pl.ds(start, size)
        dh = mm((dyh[here, :], dyl[here, :]), (vh[...], vl[...]), 1, 0)
        g, slope = gelu_parts(ub[here, :])
        a, b = split(g)
        gh[here, :] = a
        gl[here, :] = b
        ub[here, :] = dh * slope
        part[here, :] = mm(split(ub[here, :]), (wh[...], wl[...]), 1, 1)
        if start > 0:
            send_parts(copies, part, half, None, theirs)
    if last:
        send_parts(copies, part, half, mine, theirs)
    else:
        copies.start(part.at[pl.ds(0, half)], mine)
    if accumulate:
        copies.wait(*co)
    new = mm((dyh[...], dyl[...]), (gh[...], gl[...]), 0, 0)
    gdb[...] = gdb[...] + new if accumulate else new
    d_half = z.d // 2
    copies.start(gdb.at[pl.ds(0, d_half)], gdn)
    copies.start(gdb.at[pl.ds(d_half, d_half)], gdf)
    nh, _ = norm_stats(xb[...])
    new = mm(split(nh * gain), split(ub[...]), 0, 0)
    gub[...] = gub[...] + new if accumulate else new
    copies.start(gub.at[pl.ds(0, d_half)], gun)
    copies.start(gub.at[pl.ds(d_half, d_half)], guf)
    copies.wait_all()


def ffn_bwd(z, l, last, blocks, inputs, olds):
    r = z.queries if last else z.rows
    big = lambda t=F32: pltpu.VMEM((z.d, z.d), t)
    tall = lambda t=F32: pltpu.VMEM((r, z.d), t)
    scratch = [tall(), pltpu.VMEM((2 * r, z.d), F32), big(), big(BF16), big(BF16), big(), big(BF16), big(BF16)]
    scratch += [tall(), tall(), tall(BF16), tall(BF16), tall(BF16), tall(BF16), tall(), big(), big()]
    scratch += [pltpu.VMEM((8, z.d), F32)]
    specs = [VMEM] + ([VMEM] if last else [ANY]) + [ANY] * (len(inputs) - 2)
    if not last:
        scratch += [tall()]
    h = z.d // 2
    outs = [(r, z.d), (r // 2, z.d), (r // 4, z.d), (r // 4, z.d), (8, z.d)] + [(h, z.d)] * 4
    aliases = None
    if olds is not None:
        aliases = {len(inputs) + i: 5 + i for i in range(4)}
        inputs = list(inputs) + list(olds)
        specs = specs + [ANY] * 4
    return run(
        functools.partial(ffn_bwd_kernel, z, l, last, olds is not None, blocks),
        f"ffn_bwd{l}",
        inputs,
        specs,
        outs,
        scratch,
        48,
        3 * 8 * r * z.d * z.d,
        32 << 20,
        aliases,
    )


def attn_bwd_kernel(z, l, first, last, accumulate, blocks, *refs):
    (vec, dyp, xm, pa, pb, pc, pd, *weights) = refs[: 7 + blocks]
    (x_in, q_in, kv_in, o_in, lse_in, mask) = refs[7 + blocks : 13 + blocks]
    refs = refs[13 + blocks :]
    c_ref = None
    if first:
        c_ref, refs = refs[0], refs[1:]
    if accumulate:
        olds, refs = refs[:2], refs[2:]
    if first:
        dy_out, dq_out, dkv_out, gv, gn, gf = refs[:6]
        refs = refs[6:]
    else:
        dy_out, mine, *theirs, gv, gn, gf = refs[:7]
        refs = refs[7:]
    (dyb, xmb, add, wb, wh, wl, xb, qb, kvb, ob, lseb, maskb, dyh, dyl, dqb, dkb, dvb, gb, gvb, sems) = refs
    copies = Copies(sems)
    rq = z.queries if last else z.rows
    half = rq // 2
    ca = [copies.start(p, add.at[pl.ds(i * half, half)]) for i, p in enumerate((pa, pb, pc, pd))]
    ca += [copies.start(dyp, dyb), copies.start(xm, xmb)]
    cw = load_weight(copies, weights, wb, c_ref)
    cq = [copies.start(q_in, qb), copies.start(kv_in, kvb), copies.start(o_in, ob)]
    cq += [copies.start(lse_in, lseb), copies.start(mask, maskb)]
    cx = [copies.start(x_in, xb)]
    if accumulate:
        co = list(load_pair(copies, olds[0], olds[1], gb))
    gvb[...] = jnp.zeros_like(gvb)
    copies.wait(*ca)
    gain2 = row(vec, z.depth + l)
    for i in range(2):
        here = pl.ds(i * half, half)
        total = add[pl.ds(2 * i * half, half), :] + add[pl.ds((2 * i + 1) * half, half), :]
        nh, rstd = norm_stats(xmb[here, :])
        dy = dyb[here, :] + norm_back(total * gain2, nh, rstd)
        gvb[pl.ds(z.depth + l, 1), :] += z.share * jnp.sum(total * nh, axis=0, keepdims=True)
        dyb[here, :] = dy
        a, b = split(dy)
        dyh[here, :] = a
        dyl[here, :] = b
    copies.start(dyb, dy_out)
    copies.wait(*cw)
    split_into(wh, wl, wb[...])
    copies.wait(*cq)
    kh = split(kvb[:, z.k])
    vh = split(kvb[:, z.v])
    km = [keep(kh, h * HD) for h in range(z.heads)]
    dkb[...] = jnp.zeros_like(dkb)
    dvb[...] = jnp.zeros_like(dvb)
    tiles = [(0, rq)] if last else [(half, half), (0, half)]
    for start, size in tiles:
        here = pl.ds(start, size)
        do = mm((dyh[here, :], dyl[here, :]), (wh[:, z.o], wl[:, z.o]), 1, 0)
        doh = split(do)
        prod = do * ob[here, :]
        qh = split(qb[here, :])
        m_tile = maskb[...] if last else maskb[pl.ds((start // half) * z.hq, z.hq), :]
        dq = jnp.zeros((size, 256), F32)
        for h in range(z.heads):
            qm = keep(qh, h * HD)
            dm = keep(doh, HD + h * HD)
            s = scores(z, qh, kh, h, m_tile, 0 if last else z.hc)
            p = jnp.exp(s - lseb[here, h : h + 1])
            delta = jnp.sum(
                jnp.where(lanes(prod.shape, HD + h * HD), prod, 0.0), axis=-1, keepdims=True
            )
            dp = mm(dm, vh, 1, 1)
            ds = split(p * (dp - delta))
            dq = dq + mm(ds, km[h], 1, 0)
            dkb[...] += mm(ds, qm, 0, 0)
            dvb[...] += mm(split(p), dm, 0, 0)
        dqb[here, :] = dq * QSCALE
    kvb[:, 0:128] = dkb[:, 0:128]
    kvb[:, 128:256] = dkb[:, 128:256] + dvb[:, 0:128]
    kvb[:, 256:384] = dvb[:, 128:256]
    if first:
        copies.start(dqb, dq_out)
        copies.start(kvb, dkv_out)
    if accumulate:
        copies.wait(*co)
    g_out = mm((dyh[...], dyl[...]), split(ob[...]), 0, 0)
    copies.wait(*cx)
    gain = row(vec, l)
    dnb = add
    g_q = jnp.zeros((z.d, 256), F32)
    g_kv = jnp.zeros((z.d, 384), F32)
    for i in (1, 0):
        here = pl.ds(i * z.half, z.half)
        nh, rstd = norm_stats(xb[here, :])
        n = split(nh * gain)
        nc = (n[0][: z.hc], n[1][: z.hc])
        nq = (n[0][z.hc :], n[1][z.hc :]) if last else n
        qrows = pl.ds(i * z.hq, z.hq) if last else here
        dq = split(dqb[qrows, :])
        dkv = split(kvb[pl.ds(i * z.hc, z.hc), :])
        g_q = g_q + mm(nq, dq, 0, 0)
        g_kv = g_kv + mm(nc, dkv, 0, 0)
        if first:
            continue
        dn_q = mm(dq, (wh[:, z.q], wl[:, z.q]), 1, 1)
        dn_c = mm(dkv, (wh[:, z.kv], wl[:, z.kv]), 1, 1)
        if last:
            dn = jnp.concatenate([dn_c, dn_q], axis=0)
        else:
            dn = jnp.concatenate([dn_q[: z.hc] + dn_c, dn_q[z.hc :]], axis=0)
        dnb[pl.ds(i * z.half, z.half), :] = dn
        if i > 0:
            send_parts(copies, dnb, z.half, None, theirs)
        else:
            copies.start(dnb.at[here], mine)
    copies.start(gvb, gv)
    new = [
        g_kv,
        g_q[:, 0:128],
        g_q[:, 128:256] + g_out[:, 0:128],
        g_out[:, 128:256],
    ]
    at = 0
    for piece in new:
        cols = slice(at, at + piece.shape[1])
        gb[:, cols] = gb[:, cols] + piece if accumulate else piece
        at += piece.shape[1]
    d_half = z.d // 2
    copies.start(gb.at[pl.ds(0, d_half)], gn)
    copies.start(gb.at[pl.ds(d_half, d_half)], gf)
    copies.wait_all()


def attn_bwd(z, l, last, blocks, inputs, firsts, olds):
    first = l == 0
    rq = z.queries if last else z.rows
    big = lambda t=F32: pltpu.VMEM((z.d, z.d), t)
    tall = lambda t=F32: pltpu.VMEM((rq, z.d), t)
    scratch = [tall(), tall(), pltpu.VMEM((2 * z.rows, z.d), F32), big(), big(BF16), big(BF16)]
    scratch += [pltpu.VMEM((z.rows, z.d), F32), pltpu.VMEM((rq, 256), F32), pltpu.VMEM((z.context, 384), F32)]
    scratch += [pltpu.VMEM((rq, 256), F32), pltpu.VMEM((rq, 128), F32), pltpu.VMEM((z.queries, z.context), F32)]
    scratch += [tall(BF16), tall(BF16), pltpu.VMEM((rq, 256), F32)]
    scratch += [pltpu.VMEM((z.context, 256), F32), pltpu.VMEM((z.context, 256), F32), big(), pltpu.VMEM((8, z.d), F32)]
    specs = [VMEM] + [ANY] * (12 + blocks)
    h = z.d // 2
    outs = [(8, z.d), (h, z.d), (h, z.d)]
    inputs = list(inputs)
    if first:
        inputs += list(firsts)
        specs += [SMEM]
        outs = [(rq, z.d), (rq, 256), (z.context, 384)] + outs
        grads = [4, 5]
    else:
        outs = [(rq, z.d), (z.half, z.d), (z.half // 2, z.d), (z.half // 2, z.d)] + outs
        grads = [5, 6]
    aliases = None
    if olds is not None:
        aliases = {len(inputs) + i: g for i, g in enumerate(grads)}
        inputs += list(olds)
        specs += [ANY] * len(olds)
    return run(
        functools.partial(attn_bwd_kernel, z, l, first, last, olds is not None, blocks),
        f"attn_bwd{l}",
        inputs,
        specs,
        outs,
        scratch,
        48,
        3 * 2 * (4 * rq * z.d * 256 + 2 * z.context * z.d * 384 + 15 * rq * z.context * 256),
        24 << 20,
        aliases,
    )


def embed_bwd_kernel(z, accumulate, blocks, *refs):
    (c_ref, t_in, vec, feat, x_in, dy, dq, dkv, *weights) = refs[: 8 + blocks]
    refs = refs[8 + blocks :]
    if accumulate:
        old, refs = refs[0], refs[1:]
    gv, emb_out = refs[:2]
    (xb, dyb, dqb, kvb, wb, wh, wl, featb, geb, gvb, sems) = refs[2:]
    copies = Copies(sems)
    cw = load_weight(copies, weights, wb, c_ref)
    cd = [copies.start(dq, dqb), copies.start(dkv, kvb)]
    cx = [copies.start(x_in, xb), copies.start(dy, dyb)]
    cx += load_feats(copies, z, c_ref, feat, featb)
    if accumulate:
        co = copies.start(old, geb)
    gvb[...] = jnp.zeros_like(gvb)
    copies.wait(*cw)
    split_into(wh, wl, wb[...])
    copies.wait(*cd)
    copies.wait(*cx)
    gain = row(vec, 0)
    ge = 0.0
    for i in range(2):
        here = pl.ds(i * z.half, z.half)
        nh, rstd = norm_stats(xb[here, :])
        dn_q = mm(split(dqb[here, :]), (wh[:, z.q], wl[:, z.q]), 1, 1)
        dn_c = mm(split(kvb[pl.ds(i * z.hc, z.hc), :]), (wh[:, z.kv], wl[:, z.kv]), 1, 1)
        dn = jnp.concatenate([dn_q[: z.hc] + dn_c, dn_q[z.hc :]], axis=0)
        gvb[pl.ds(0, 1), :] += jnp.sum(dn * nh, axis=0, keepdims=True)
        dx = z.share * dyb[here, :] + norm_back(dn * gain, nh, rstd)
        gvb[pl.ds(2 * z.depth + 1, 1), :] += jnp.sum(dx * t_in[here, :], axis=0, keepdims=True)
        ge = ge + mm(split(dx), split(featb[here, :]), 0, 0)
    copies.start(gvb, gv)
    if accumulate:
        copies.wait(co)
        ge = geb[...] + ge
    geb[...] = ge
    copies.start(geb, emb_out)
    copies.wait_all()


def embed_bwd(z, blocks, inputs, old):
    big = lambda t=F32: pltpu.VMEM((z.d, z.d), t)
    scratch = [pltpu.VMEM((z.rows, z.d), F32), pltpu.VMEM((z.rows, z.d), F32), pltpu.VMEM((z.rows, 256), F32)]
    scratch += [pltpu.VMEM((z.context, 384), F32), big(), big(BF16), big(BF16)]
    scratch += [pltpu.VMEM((z.rows, z.feats), F32), pltpu.VMEM((z.d, z.feats), F32), pltpu.VMEM((8, z.d), F32)]
    specs = [SMEM, VMEM, VMEM] + [ANY] * (5 + blocks)
    aliases = None
    if old is not None:
        aliases = {len(inputs): 1}
        inputs = list(inputs) + [old]
        specs = specs + [ANY]
    return run(
        functools.partial(embed_bwd_kernel, z, old is not None, blocks),
        "embed_bwd",
        inputs,
        specs,
        [(8, z.d), (z.d, z.feats)],
        scratch,
        48,
        3 * 2 * (z.rows * z.d * 256 + z.context * z.d * 384 + z.rows * z.d * z.feats),
        12 << 20,
        aliases,
    )


def roll_half(x, c):
    half = x.shape[0] // 2
    return jnp.where(c == 0, x, jnp.concatenate([x[half:], x[:half]], axis=0))


def interleave(ctx, qry):
    hc, hq = ctx.shape[0] // 2, qry.shape[0] // 2
    return jnp.concatenate([ctx[:hc], qry[:hq], ctx[hc:], qry[hq:]], axis=0)


def neighbour_mask(neigh, live, context_rows, c):
    words = context_rows // 32
    col = jnp.bitwise_xor(neigh, c * (context_rows // 2))
    bit = jnp.left_shift(live, jnp.bitwise_and(col, 31))
    at = jnp.right_shift(col, 5)
    index = jnp.arange(words, dtype=jnp.int32)[None, :, None]
    word = jnp.sum(jnp.where(at[:, None, :] == index, bit[:, None, :], 0), axis=-1)
    spread = jnp.broadcast_to(word[:, :, None], word.shape + (32,)).reshape(word.shape[0], context_rows)
    shift = jnp.bitwise_and(jnp.arange(context_rows, dtype=jnp.int32), 31)
    return jnp.bitwise_and(jnp.right_shift(spread, shift[None, :]), 1).astype(F32)


def adamw(weight, grad, first, second, rate, decay, steps_taken):
    first_new = 0.9 * first + 0.1 * grad
    second_new = 0.999 * second + 0.001 * grad * grad
    first_hat = first_new / (1.0 - jnp.power(0.9, steps_taken))
    second_hat = second_new / (1.0 - jnp.power(0.999, steps_taken))
    weight_new = weight - rate * (first_hat / (jnp.sqrt(second_hat) + 1e-08) + decay * weight)
    return (weight_new, first_new, second_new)


def on_device(
    features,
    targets,
    neighbours,
    nbr_mask,
    flags,
    step_count,
    w_qkv,
    w_out,
    w_up,
    w_down,
    emb_weight,
    vectors,
    m_qkv,
    m_out,
    m_up,
    m_down,
    m_emb,
    m_vectors,
    v_qkv,
    v_out,
    v_up,
    v_down,
    v_emb,
    v_vectors,
):
    depth, d_rows = w_qkv.shape[:2]
    micros, _, rows, feats = features.shape
    queries = neighbours.shape[2]
    context = rows - queries
    width = w_qkv.shape[2] // 3
    d = d_rows * lax.axis_size("dh") * lax.axis_size("dl")
    share = 1.0 / (lax.axis_size("hh") * lax.axis_size("hl"))
    z = Sizes(d, context, queries, depth, width, feats, share)
    c = lax.axis_index("hl")
    c_arr = jnp.stack([c, lax.axis_index("dh")]).astype(jnp.int32)

    zi = lax.axis_index("dh")
    line = lax.axis_size("dh")
    near_by = line == 4

    def hop(value, step):
        return lax.ppermute(value, "dh", [(i, i ^ step) for i in range(line)])

    own_rows = jnp.concatenate([emb_weight, vectors], axis=1)
    if near_by:
        b0, b1, b2, b3 = [own_rows] + [hop(own_rows, m) for m in (1, 2, 3)]
        odd, high = jnp.bitwise_and(zi, 1) == 1, zi >= 2
        b0, b1 = jnp.where(odd, b1, b0), jnp.where(odd, b0, b1)
        b2, b3 = jnp.where(odd, b3, b2), jnp.where(odd, b2, b3)
        near = [jnp.where(high, b2, b0), jnp.where(high, b3, b1), jnp.where(high, b0, b2), jnp.where(high, b1, b3)]
        near = jnp.concatenate(near, axis=0)
        far = swap(near, "dl")
    else:
        near, far = gather_rows(own_rows)
    small = jnp.concatenate([near, far], axis=0)
    emb = small[:, :feats]
    vec = jnp.pad(small[:, feats:].T, ((0, 1), (0, 0)))
    def rows_near(block):
        return lax.all_gather(block, "dh", axis=0, tiled=True)

    blocks = []
    for l in range(depth):
        parts = [w_qkv[l][:, width:], w_qkv[l][:, :width], w_out[l]]
        blocks += [jnp.concatenate(parts, axis=1), w_up[l], w_down[l]]

    tables = []
    for m in range(micros):
        t_ctx = roll_half(targets[m, 0][:context], c)
        t_qry = roll_half(targets[m, 0][context:], c)
        t_in = interleave(t_ctx, jnp.zeros((queries,), F32))[:, None]
        flag = roll_half(flags[m, 0], c).astype(F32)
        mask = neighbour_mask(roll_half(neighbours[m, 0], c), roll_half(nbr_mask[m, 0], c), context, c)
        tables.append(dict(feat=features[m, 0], t_in=t_in, side=jnp.stack([flag, t_qry], axis=1), mask=mask))

    held, pending = [vec], []

    def beside(kernel, *transfers, ahead=(), strict=False):
        gate = after(held[0], *ahead)
        moved = [t() for t in transfers]
        outs = list(kernel(gate))
        moved = [after(x, outs[0]) for x in moved]
        held[0] = after(vec, *moved)
        for pieces in pending:
            pieces.append(swap(after(pieces[1], outs[0]), "hl"))
        pending.clear()
        if strict:
            outs[-1] = after(outs[-1], *moved)
        return (outs, *moved)

    def sent(pieces):
        held[0] = after(held[0], pieces[0])
        came[0] = pieces[1]
        pending.append(pieces)
        return pieces

    came = [None]
    near, far = [None] * len(blocks), [None] * len(blocks)

    def gather(i):
        return lambda: rows_near(blocks[i])

    def cross(i, part=None):
        if part is None:
            return lambda: swap(near[i], "dl")
        half = near[i].shape[0] // 2
        return lambda: swap(near[i][part * half : (part + 1) * half], "dl")

    def both(i):
        return near[i] if isinstance(near[i], tuple) else (near[i], far[i])

    def held_blocks(*indices):
        return tuple(len(both(i)) for i in indices)

    saved = [[None] * depth for _ in range(micros)]
    state = [None] * micros

    def attn_forward(l, m, *transfers, ahead=(), strict=False):
        t, last = tables[m], l == depth - 1

        def call(gate):
            if l == 0:
                inputs = (c_arr, t["t_in"], gate, t["feat"], emb, *both(0), t["mask"])
            else:
                inputs = (gate, state[m][0], *state[m][1], *both(3 * l), t["mask"])
            return attn_fwd(z, l, last, *held_blocks(3 * l), inputs)

        (x, q, kv, o, lse, mine, *theirs), *moved = beside(call, *transfers, ahead=ahead, strict=strict)
        saved[m][l] = dict(x=x, q=q, kv=kv, o=o, lse=lse)
        state[m] = (x, sent(head_sum(mine, theirs, came[0])))
        return moved

    def ffn_forward(l, m, *transfers, ahead=(), strict=False):
        def call(gate):
            inputs = (gate, state[m][0], *state[m][1], *both(3 * l + 1), *both(3 * l + 2))
            return ffn_fwd(z, l, l == depth - 1, held_blocks(3 * l + 1, 3 * l + 2), inputs)

        (x1, u, mine, *theirs), *moved = beside(call, *transfers, ahead=ahead, strict=strict)
        saved[m][l].update(x1=x1, u=u)
        state[m] = (x1, sent(head_sum(mine, theirs, came[0])))
        return moved

    if near_by:
        first = [blocks[0]] + [hop(blocks[0], m) for m in (1, 2, 3)]
        near[0] = tuple(first + [swap(block, "dl") for block in first])
        near[2] = (rows_near(jnp.concatenate([blocks[2], swap(blocks[2], "dl")], axis=0)),)
    else:
        near[0] = gather_rows(blocks[0])
        near[2] = gather_rows(blocks[2])
    near[1] = rows_near(blocks[1])
    attn_forward(0, 0, ahead=(near[1],))
    (far[1],) = attn_forward(0, 1, cross(1), strict=True)
    (near[3],) = ffn_forward(0, 0, gather(3))
    far[3], near[4] = ffn_forward(0, 1, cross(3), gather(4))
    far[4], near[5] = attn_forward(1, 0, cross(4), gather(5))
    (far[5],) = attn_forward(1, 1, cross(5), strict=True)
    ffn_forward(1, 0)
    ffn_forward(1, 1)

    g_attn, g_ffn = [None] * depth, [None] * depth
    g_vecs = []
    cot = [None] * micros

    def ffn_backward(l, m, *transfers):
        k, last = saved[m][l], l == depth - 1

        def call(gate):
            weights = (k["u"], *both(3 * l + 1), *both(3 * l + 2))
            if last:
                inputs = (gate, tables[m]["side"], k["x1"], *state[m][1], *weights)
            else:
                res, pieces = cot[m]
                inputs = (gate, res, saved[m][l + 1]["x"], k["x1"], *pieces, *weights)
            return ffn_bwd(z, l, last, held_blocks(3 * l + 1, 3 * l + 2), inputs, g_ffn[l])

        (dy, mine, t0, t1, gv, *g_ffn[l]), *moved = beside(call, *transfers)
        g_vecs.append(gv)
        cot[m] = (dy, sent(head_sum(mine, (t0, t1), came[0])))
        return moved

    def attn_backward(l, m, *transfers):
        k, t, last = saved[m][l], tables[m], l == depth - 1

        def call(gate):
            dy, pieces = cot[m]
            inputs = (gate, dy, k["x1"], *pieces, *both(3 * l), k["x"], k["q"], k["kv"], k["o"], k["lse"], t["mask"])
            firsts = (c_arr,) if l == 0 else ()
            return attn_bwd(z, l, last, *held_blocks(3 * l), inputs, firsts, g_attn[l])

        outs, *moved = beside(call, *transfers)
        if l == 0:
            *cot[m], gv, g_near, g_far = outs
            g_attn[l] = [g_near, g_far]
        else:
            dy, mine, t0, t1, gv, *g_attn[l] = outs
            cot[m] = (dy, sent(head_sum(mine, (t0, t1), came[0])))
        g_vecs.append(gv)
        return moved

    def cross_far(pair):
        return lambda: swap(pair[1], "dl")

    def reduce(part):
        return lambda: scatter_near(part)

    ffn_backward(1, 0)
    ffn_backward(1, 1)
    up1, down1 = g_ffn[1][:2], g_ffn[1][2:]
    attn_backward(1, 0)
    (got,) = attn_backward(1, 1, cross_far(up1))
    own_up1 = up1[0] + got
    packed1 = g_attn[1][:2]
    got, own_up1 = ffn_backward(0, 0, cross_far(down1), reduce(own_up1))
    own_down1 = down1[0] + got
    got, own_down1 = ffn_backward(0, 1, cross_far(packed1), reduce(own_down1))
    own_packed1 = packed1[0] + got
    up0, down0 = g_ffn[0][:2], g_ffn[0][2:]
    got, own_packed1 = attn_backward(0, 0, cross_far(up0), reduce(own_packed1))
    own_up0 = up0[0] + got
    got, own_up0 = attn_backward(0, 1, cross_far(down0), reduce(own_up0))
    own_down0 = down0[0] + got

    g_emb = [None]

    def embed_backward(m, *transfers):
        t = tables[m]

        def call(gate):
            inputs = (c_arr, t["t_in"], gate, t["feat"], saved[m][0]["x"], *cot[m], *both(0))
            return embed_bwd(z, *held_blocks(0), inputs, g_emb[0])

        (gv, g_emb[0]), *moved = beside(call, *transfers)
        g_vecs.append(gv)
        return moved

    packed0 = g_attn[0]
    got = swap(after(packed0[1], own_down0), "dl")
    own_down0 = scatter_near(own_down0)
    embed_backward(0)
    embed_backward(1)
    own_down0 = after(own_down0, g_vecs[-1])
    own_packed0 = scatter_near(packed0[0] + after(got, g_vecs[-1]))
    own = [[own_packed0, own_packed1], [own_up0, own_up1], [own_down0, own_down1]]

    owned = [
        jnp.stack([jnp.concatenate([o[:, 2 * width : 3 * width], o[:, : 2 * width]], axis=1) for o in own[0]]),
        jnp.stack([o[:, 3 * width :] for o in own[0]]),
        jnp.stack(own[1]),
        jnp.stack(own[2]),
    ]
    n_vec = vectors.shape[1]
    g_vec = sum(g_vecs[1:], g_vecs[0])
    loss_local = share * g_vec[n_vec, 0]
    g_small = jnp.concatenate([g_emb[0], g_vec[:n_vec].T], axis=1)
    own_small = near_rows(g_small[: d // 2], g_small[d // 2 :])
    if near_by:
        piece = lambda m: lax.dynamic_slice_in_dim(own_small, jnp.bitwise_xor(zi, m) * d_rows, d_rows, axis=0)
        own_small = (piece(0) + hop(piece(1), 1)) + (hop(piece(2), 2) + hop(piece(3), 3))
    else:
        own_small = scatter_near(own_small)
    own_small = own_small + swap(own_small, "hl")
    own_small = own_small + swap(own_small, "hh")
    own_emb, own_vec = own_small[:, :feats], own_small[:, feats:]
    owned += [own_emb, own_vec]

    squares = share * jnp.sum(own_small * own_small)
    for o in owned[:4]:
        squares = squares + jnp.sum(o * o)
    counted = share * jnp.sum(flags.astype(F32))
    sums = everyone_sum(jnp.stack([squares, loss_local, counted]))
    counted = jnp.maximum(sums[2], 1.0)
    loss = sums[1] / counted
    grad_norm = jnp.sqrt(sums[0]) / counted
    factor = CLIP_AT / jnp.maximum(grad_norm, CLIP_AT) / counted
    steps_taken = step_count[0].astype(F32)
    weights = (w_qkv, w_out, w_up, w_down, emb_weight, vectors)
    firsts = (m_qkv, m_out, m_up, m_down, m_emb, m_vectors)
    seconds = (v_qkv, v_out, v_up, v_down, v_emb, v_vectors)
    new_w, new_m, new_v = [], [], []
    for i in range(6):
        rate = LR_VECTOR if i == 5 else LR_MATRIX
        decay = 0.0 if i == 5 else DECAY
        result = adamw(weights[i], owned[i] * factor, firsts[i], seconds[i], rate, decay, steps_taken)
        new_w.append(result[0])
        new_m.append(result[1])
        new_v.append(result[2])
    return (loss, grad_norm, *new_w, *new_m, *new_v)


def solution(mesh):
    dp, head = mesh.shape["dp"], mesh.shape["head"]
    fine = Mesh(mesh.devices.reshape(dp // 2, 2, head // 2, 2), AXES)
    rows, cols = ("dh", "dl"), ("hh", "hl")
    data = (
        P(None, rows, None, None),
        P(None, rows, None),
        P(None, rows, None, None),
        P(None, rows, None, None),
        P(None, rows, None),
        P(),
    )
    params = (P(None, rows, cols),) * 4 + (P(rows, None),) * 2
    return jax.shard_map(
        on_device,
        mesh=fine,
        in_specs=data + params * 3,
        out_specs=(P(), P()) + params * 3,
        check_vma=False,
    )
```

```python
import functools

import jax
import jax.numpy as jnp
from jax import lax
from jax.experimental import pallas as pl
from jax.experimental.pallas import tpu as pltpu
from jax.sharding import Mesh, PartitionSpec as P

HD = 64
LR_MATRIX = 0.03
LR_VECTOR = 0.2
DECAY = 0.1
CLIP_AT = 0.02
EPS = 1e-05
SWAP = ((0, 1), (1, 0))
AXES = ("dh", "dl", "hh", "hl")
F32, BF16 = jnp.float32, jnp.bfloat16
ANY = pl.BlockSpec(memory_space=pl.ANY)
SMEM = pl.BlockSpec(memory_space=pltpu.SMEM)
VMEM = pl.BlockSpec(memory_space=pltpu.VMEM)
QSCALE = HD ** (-0.5)
COST = 20


def swap(values, axis):
    return lax.ppermute(values, axis, SWAP)


def head_sum(mine, theirs, before=None):
    if before is not None and before.shape[0] < mine.shape[0]:
        theirs, before = [after(t, before) for t in theirs], None
    first, second = (swap(t, "hl") for t in theirs)
    a = mine + jnp.concatenate([after(first, before), second], axis=0)
    return [a, swap(a, "hh"), swap(a, "hl")]


def gather_rows(block):
    near = lax.all_gather(block, "dh", axis=0, tiled=True)
    return near, swap(near, "dl")


def everyone_sum(values):
    values = jnp.broadcast_to(jnp.pad(values, (0, 128 - values.shape[0]))[None], (8, 128))
    for axis in ("hl", "hh", "dl"):
        values = values + swap(values, axis)
    size = lax.axis_size("dh")
    if size & (size - 1):
        return lax.psum(values, "dh")[0]
    step = 1
    while step < size:
        values = values + lax.ppermute(values, "dh", [(i, i ^ step) for i in range(size)])
        step *= 2
    return values[0]


def near_rows(near, far):
    return near + swap(far, "dl")


def scatter_near(near):
    return lax.psum_scatter(near, "dh", scatter_dimension=0, tiled=True)


def after(value, *others):
    others = [o for o in others if o is not None]
    return lax.optimization_barrier((value, *others))[0] if others else value


def split(a):
    hi = a.astype(BF16)
    return hi, (a - hi.astype(F32)).astype(BF16)


def dg(a, b, ca, cb):
    return lax.dot_general(a, b, (((ca,), (cb,)), ((), ())), preferred_element_type=F32)


def mm(a, b, ca, cb):
    return (dg(a[1], b[0], ca, cb) + dg(a[0], b[1], ca, cb)) + dg(a[0], b[0], ca, cb)


def norm_stats(x):
    centre = x - jnp.mean(x, axis=-1, keepdims=True)
    rstd = lax.rsqrt(jnp.mean(centre * centre, axis=-1, keepdims=True) + EPS)
    return centre * rstd, rstd


def norm_back(dn, nh, rstd):
    return rstd * (
        dn - jnp.mean(dn, axis=-1, keepdims=True) - nh * jnp.mean(dn * nh, axis=-1, keepdims=True)
    )


def gelu_parts(u):
    t = jnp.tanh(0.7978845608 * (u + 0.044715 * u * u * u))
    value = 0.5 * u * (1.0 + t)
    slope = 0.5 * (1.0 + t) + 0.5 * u * (1.0 - t * t) * 0.7978845608 * (1.0 + 3.0 * 0.044715 * u * u)
    return value, slope


def lanes(shape, low):
    at = lax.broadcasted_iota(jnp.int32, shape, 1)
    return (at >= low) & (at < low + HD)


def keep(pair, low):
    held = lanes(pair[0].shape, low)
    zero = jnp.zeros(pair[0].shape, BF16)
    return jnp.where(held, pair[0], zero), jnp.where(held, pair[1], zero)


class Copies:
    def __init__(self, sems):
        self.sems, self.count, self.open = sems, 0, []

    def start(self, src, dst):
        copy = pltpu.make_async_copy(src, dst, self.sems.at[self.count])
        self.count += 1
        copy.start()
        self.open.append(copy)
        return copy

    def wait(self, *copies):
        for copy in copies:
            copy.wait()
            self.open = [other for other in self.open if other is not copy]

    def wait_all(self):
        self.wait(*list(self.open))


def load_pair(copies, near, far, dst):
    half = near.shape[0]
    return (
        copies.start(near, dst.at[pl.ds(0, half)]),
        copies.start(far, dst.at[pl.ds(half, half)]),
    )


def load_halves(copies, x, xb, pieces, add):
    half = xb.shape[0] // 2
    made = []
    for i in range(2):
        here = pl.ds(i * half, half)
        group = [copies.start(x[i] if isinstance(x, tuple) else x.at[here], xb.at[here])]
        for j in (2 * i, 2 * i + 1):
            group.append(copies.start(pieces[j], add.at[pl.ds(j * half, half)]))
        made.append(group)
    return made


def send_parts(copies, part, half, mine, theirs):
    quarter = half // 2
    for i, piece in enumerate(theirs):
        copies.start(part.at[pl.ds(half + i * quarter, quarter)], piece)
    if mine is not None:
        copies.start(part.at[pl.ds(0, half)], mine)


def load_weight(copies, arrays, dst, z_ref=None):
    if len(arrays) == 2:
        return load_pair(copies, arrays[0], arrays[1], dst)
    rows = dst.shape[0] // 8
    made = []
    for i in range(8):
        if len(arrays) == 1:
            src = arrays[0].at[pl.ds(((i % 4) * 2 + i // 4) * rows, rows)]
            at = i * rows
        else:
            src = arrays[i]
            at = pl.multiple_of((i // 4 * 4 + jnp.bitwise_xor(z_ref[1], i % 4)) * rows, 8)
        made.append(copies.start(src, dst.at[pl.ds(at, rows)]))
    return tuple(made)


def row(vec_ref, index):
    return vec_ref[pl.ds(index, 1), :]


def run(kernel, name, inputs, specs, outs, scratch, sems, flops, moved, aliases=None):
    return pl.pallas_call(
        kernel,
        name=name,
        out_shape=[jax.ShapeDtypeStruct(s, F32) for s in outs],
        in_specs=specs,
        out_specs=[ANY] * len(outs),
        scratch_shapes=list(scratch) + [pltpu.SemaphoreType.DMA((sems,))],
        input_output_aliases=aliases or {},
        compiler_params=pltpu.CompilerParams(vmem_limit_bytes=56 << 20),
        cost_estimate=pl.CostEstimate(flops=flops // COST, bytes_accessed=moved // COST, transcendentals=0),
    )(*inputs)


class Sizes:
    def __init__(self, d, context, queries, depth, width, feats, share):
        self.d, self.context, self.queries = d, context, queries
        self.depth, self.width, self.feats, self.share = depth, width, feats, share
        self.hc, self.hq = context // 2, queries // 2
        self.half = self.hc + self.hq
        self.rows = context + queries
        self.heads = width // HD
        self.k = slice(0, 256)
        self.v = slice(128, 384)
        self.q = slice(384, 640)
        self.o = slice(512, 768)
        self.kv = slice(0, 384)


def load_feats(copies, z, c_ref, feat, dst):
    c = c_ref[0]
    made = []
    for i in range(2):
        side = c if i == 0 else 1 - c
        made.append(
            copies.start(
                feat.at[pl.ds(pl.multiple_of(side * z.hc, z.hc), z.hc)],
                dst.at[pl.ds(i * z.half, z.hc)],
            )
        )
        made.append(
            copies.start(
                feat.at[pl.ds(pl.multiple_of(z.context + side * z.hq, z.hq), z.hq)],
                dst.at[pl.ds(i * z.half + z.hc, z.hq)],
            )
        )
    return made


def split_into(hi, lo, value):
    a, b = split(value)
    hi[...] = a
    lo[...] = b


def scores(z, qh, kh, h, mask, masked_from):
    s = mm(keep(qh, h * HD), kh, 1, 1)
    if masked_from == 0:
        return jnp.where(mask > 0, s, -1e30)
    low = jnp.where(mask > 0, s[masked_from:], -1e30)
    return jnp.concatenate([s[:masked_from], low], axis=0)


def attn_fwd_kernel(z, l, first, last, blocks, *refs):
    c_ref = None
    if first:
        (c_ref, t_in, vec, feat, emb, *weights, mask) = refs[: 6 + blocks]
        refs = refs[6 + blocks :]
    else:
        (vec, xp, pa, pb, pc, pd, *weights, mask) = refs[:9]
        refs = refs[9:]
    x_out, q_out, kv_out, o_out, lse_out, mine, *theirs = refs[:8]
    (xb, wb, wh, wl, qb, kvb, ob, lseb, part, maskb, *rest, sems) = refs[8:]
    copies = Copies(sems)
    if first:
        featb, embb = rest
        cf = load_feats(copies, z, c_ref, feat, featb)
        ce = copies.start(emb, embb)
    else:
        (add,) = rest
        cx = copies.start(xp, xb)
        ca = [
            copies.start(p, add.at[pl.ds(i * z.half, z.half)]) for i, p in enumerate((pa, pb, pc, pd))
        ]
    cw = load_weight(copies, weights, wb, c_ref)
    cm = copies.start(mask, maskb)
    if first:
        copies.wait(*cf, ce)
        embs = split(embb[...])
    else:
        copies.wait(cx, *ca)
    gain = row(vec, l)
    outs = []
    for i in range(2):
        here = pl.ds(i * z.half, z.half)
        if first:
            x = mm(split(featb[here, :]), embs, 1, 1) + t_in[here, :] * row(vec, 2 * z.depth + 1)
        else:
            x = xb[here, :] + (
                add[pl.ds(2 * i * z.half, z.half), :] + add[pl.ds((2 * i + 1) * z.half, z.half), :]
            )
        xb[here, :] = x
        outs.append(copies.start(xb.at[here], x_out.at[here]))
    copies.wait(*cw)
    split_into(wh, wl, wb[...])
    for i in range(2):
        here = pl.ds(i * z.half, z.half)
        nh, _ = norm_stats(xb[here, :])
        n = split(nh * gain)
        nc = (n[0][: z.hc], n[1][: z.hc])
        nq = (n[0][z.hc :], n[1][z.hc :]) if last else n
        qrows = pl.ds(i * z.hq, z.hq) if last else here
        qb[qrows, :] = mm(nq, (wh[:, z.q], wl[:, z.q]), 1, 0) * QSCALE
        kvb[pl.ds(i * z.hc, z.hc), :] = mm(nc, (wh[:, z.kv], wl[:, z.kv]), 1, 0)
    copies.start(qb, q_out)
    copies.start(kvb, kv_out)
    copies.wait(cm)
    kh = split(kvb[:, z.k])
    vh = split(kvb[:, z.v])
    vm = [keep(vh, HD + h * HD) for h in range(z.heads)]
    tiles = [(0, 2 * z.hq)] if last else [(z.half, z.half), (0, z.half)]
    for start, size in tiles:
        here = pl.ds(start, size)
        qh = split(qb[here, :])
        m_tile = maskb[...] if last else maskb[pl.ds((start // z.half) * z.hq, z.hq), :]
        o = jnp.zeros((size, 256), F32)
        lse = jnp.zeros((size, 128), F32)
        at = lax.broadcasted_iota(jnp.int32, (size, 128), 1)
        for h in range(z.heads):
            s = scores(z, qh, kh, h, m_tile, 0 if last else z.hc)
            top = jnp.max(s, axis=-1, keepdims=True)
            e = jnp.exp(s - top)
            total = jnp.sum(e, axis=-1, keepdims=True)
            o = o + mm(split(e), vm[h], 1, 0) * (1.0 / total)
            lse = jnp.where(at == h, top + jnp.log(total), lse)
        ob[here, :] = o
        lseb[here, :] = lse
        part[here, :] = mm(split(o), (wh[:, z.o], wl[:, z.o]), 1, 1)
        if start > 0:
            send_parts(copies, part, z.half, None, theirs)
    if last:
        send_parts(copies, part, z.hq, mine, theirs)
    else:
        copies.start(part.at[pl.ds(0, z.half)], mine)
    copies.start(ob, o_out)
    copies.start(lseb, lse_out)
    copies.wait_all()


def attn_fwd(z, l, last, blocks, inputs):
    first = l == 0
    rq = z.queries if last else z.rows
    scratch = [
        pltpu.VMEM((z.rows, z.d), F32),
        pltpu.VMEM((z.d, z.d), F32),
        pltpu.VMEM((z.d, z.d), BF16),
        pltpu.VMEM((z.d, z.d), BF16),
        pltpu.VMEM((rq, 256), F32),
        pltpu.VMEM((z.context, 384), F32),
        pltpu.VMEM((rq, 256), F32),
        pltpu.VMEM((rq, 128), F32),
        pltpu.VMEM((rq, z.d), F32),
        pltpu.VMEM((z.queries, z.context), F32),
    ]
    if first:
        scratch += [pltpu.VMEM((z.rows, z.feats), F32), pltpu.VMEM((z.d, z.feats), F32)]
        specs = [SMEM, VMEM, VMEM] + [ANY] * (3 + blocks)
    else:
        scratch += [pltpu.VMEM((4 * z.half, z.d), F32)]
        specs = [VMEM] + [ANY] * 8
    outs = [
        (z.rows, z.d),
        (rq, 256),
        (z.context, 384),
        (rq, 256),
        (rq, 128),
        (rq // 2, z.d),
        (rq // 4, z.d),
        (rq // 4, z.d),
    ]
    return run(
        functools.partial(attn_fwd_kernel, z, l, first, last, blocks),
        f"attn_fwd{l}",
        inputs,
        specs,
        outs,
        scratch,
        48,
        3 * 2 * (2 * rq * z.d * 256 + z.context * z.d * 384 + 6 * rq * z.context * 256),
        16 << 20,
    )


def ffn_fwd_kernel(z, l, last, blocks, *refs):
    (vec, xp, pa, pb, pc, pd, *weights) = refs[: 6 + sum(blocks)]
    refs = refs[6 + sum(blocks) :]
    ups, downs = weights[: blocks[0]], weights[blocks[0] :]
    x_out, u_out, mine, *theirs = refs[:5]
    (xb, add, wb, wh, wl, vb, vh, vl, ub, part, sems) = refs[5:]
    copies = Copies(sems)
    half = z.hq if last else z.half
    if last:
        xp = (xp.at[pl.ds(z.hc, z.hq)], xp.at[pl.ds(z.half + z.hc, z.hq)])
    halves = load_halves(copies, xp, xb, (pa, pb, pc, pd), add)
    cu = load_weight(copies, ups, wb)
    cd = load_weight(copies, downs, vb)
    gain = row(vec, z.depth + l)
    for i in range(2):
        here = pl.ds(i * half, half)
        copies.wait(*halves[i])
        xb[here, :] = xb[here, :] + (
            add[pl.ds(2 * i * half, half), :] + add[pl.ds((2 * i + 1) * half, half), :]
        )
    copies.start(xb, x_out)
    copies.wait(*cu)
    split_into(wh, wl, wb[...])
    tiles = [(0, 2 * half)] if last else [(half, half), (0, half)]
    for start, size in tiles:
        here = pl.ds(start, size)
        nh, _ = norm_stats(xb[here, :])
        u = mm(split(nh * gain), (wh[...], wl[...]), 1, 0)
        ub[here, :] = u
        copies.start(ub.at[here], u_out.at[here])
        if cd:
            copies.wait(*cd)
            split_into(vh, vl, vb[...])
            cd = None
        g, _ = gelu_parts(u)
        part[here, :] = mm(split(g), (vh[...], vl[...]), 1, 1)
        if start > 0:
            send_parts(copies, part, half, None, theirs)
    if last:
        send_parts(copies, part, half, mine, theirs)
    else:
        copies.start(part.at[pl.ds(0, half)], mine)
    copies.wait_all()


def ffn_fwd(z, l, last, blocks, inputs):
    r = z.queries if last else z.rows
    big = lambda t=F32: pltpu.VMEM((z.d, z.d), t)
    tall = lambda: pltpu.VMEM((r, z.d), F32)
    return run(
        functools.partial(ffn_fwd_kernel, z, l, last, blocks),
        f"ffn_fwd{l}",
        inputs,
        [VMEM] + [ANY] * (5 + sum(blocks)),
        [(r, z.d), (r, z.d), (r // 2, z.d), (r // 4, z.d), (r // 4, z.d)],
        [tall(), pltpu.VMEM((2 * r, z.d), F32), big(), big(BF16), big(BF16), big(), big(BF16), big(BF16), tall(), tall()],
        48,
        3 * 4 * r * z.d * z.d,
        24 << 20,
    )


def ffn_bwd_kernel(z, l, last, accumulate, blocks, *refs):
    held = sum(blocks)
    if last:
        (vec, side, xm, pa, pb, pc, pd, u_in, *weights) = refs[: 8 + held]
        refs = refs[8 + held :]
    else:
        (vec, res, xn, xm, pa, pb, pc, pd, u_in, *weights) = refs[: 9 + held]
        refs = refs[9 + held :]
    ups, downs = weights[: blocks[0]], weights[blocks[0] :]
    if accumulate:
        olds, refs = refs[:4], refs[4:]
    dy_out, mine, *theirs, gv, gun, guf, gdn, gdf = refs[:9]
    (xb, add, wb, wh, wl, vb, vh, vl, ub, dyb, dyh, dyl, gh, gl, part, gub, gdb, gvb, *rest, sems) = refs[9:]
    copies = Copies(sems)
    r = z.queries if last else z.rows
    half = r // 2
    pieces = (pa, pb, pc, pd)
    if last:
        halves = load_halves(copies, xm, xb, pieces, add)
    else:
        (xnb,) = rest
        halves = load_halves(copies, xn, xnb, pieces, add)
        halves[1].append(copies.start(xm, xb))
        for i in range(2):
            target = dyb.at[pl.ds(i * z.half + z.hc, z.hq)]
            halves[i].append(copies.start(res.at[pl.ds(i * z.hq, z.hq)], target))
    cd = load_weight(copies, downs, vb)
    cu_in = copies.start(u_in, ub)
    cu = load_weight(copies, ups, wb)
    cx = []
    if accumulate:
        co = (*load_pair(copies, olds[0], olds[1], gub), *load_pair(copies, olds[2], olds[3], gdb))
    gvb[...] = jnp.zeros_like(gvb)
    for i in range(2):
        here = pl.ds(i * half, half)
        copies.wait(*halves[i])
        total = add[pl.ds(2 * i * half, half), :] + add[pl.ds((2 * i + 1) * half, half), :]
        if last:
            x4 = xb[here, :] + total
            nh, rstd = norm_stats(x4)
            r_head = row(vec, 2 * z.depth + 2)
            gain = row(vec, 2 * z.depth)
            nf = nh * gain
            flag = side[here, 0:1]
            err = jnp.sum(nf * r_head, axis=-1, keepdims=True) - side[here, 1:2]
            dpred = 2.0 * flag * err
            dnf = dpred * r_head
            dy = norm_back(dnf * gain, nh, rstd)
            gvb[pl.ds(2 * z.depth + 2, 1), :] += z.share * jnp.sum(nf * dpred, axis=0, keepdims=True)
            gvb[pl.ds(2 * z.depth, 1), :] += z.share * jnp.sum(dnf * nh, axis=0, keepdims=True)
            gvb[pl.ds(7, 1), :] += jnp.broadcast_to(
                jnp.sum(flag * err * err, axis=0, keepdims=True), (1, z.d)
            )
        else:
            gain = row(vec, l + 1)
            nh, rstd = norm_stats(xnb[here, :])
            dy = norm_back(total * gain, nh, rstd)
            dy = jnp.concatenate([dy[: z.hc], dy[z.hc :] + dyb[pl.ds(i * z.half + z.hc, z.hq), :]], axis=0)
            gvb[pl.ds(l + 1, 1), :] += z.share * jnp.sum(total * nh, axis=0, keepdims=True)
        dyb[here, :] = dy
        a, b = split(dy)
        dyh[here, :] = a
        dyl[here, :] = b
    copies.start(dyb, dy_out)
    copies.start(gvb, gv)
    copies.wait(*cd)
    split_into(vh, vl, vb[...])
    if not last:
        copies.wait(*cu)
        split_into(wh, wl, wb[...])
        cu = None
    copies.wait(cu_in)
    gain = row(vec, z.depth + l)
    tiles = [(0, r)] if last else [(half, half), (0, half)]
    for start, size in tiles:
        here = pl.ds(start, size)
        dh = mm((dyh[here, :], dyl[here, :]), (vh[...], vl[...]), 1, 0)
        g, slope = gelu_parts(ub[here, :])
        a, b = split(g)
        gh[here, :] = a
        gl[here, :] = b
        ub[here, :] = dh * slope
        if cu:
            copies.wait(*cu)
            split_into(wh, wl, wb[...])
            cu = None
        part[here, :] = mm(split(ub[here, :]), (wh[...], wl[...]), 1, 1)
        if start > 0:
            send_parts(copies, part, half, None, theirs)
    if last:
        send_parts(copies, part, half, mine, theirs)
    else:
        copies.start(part.at[pl.ds(0, half)], mine)
    if accumulate:
        copies.wait(*co)
    new = mm((dyh[...], dyl[...]), (gh[...], gl[...]), 0, 0)
    gdb[...] = gdb[...] + new if accumulate else new
    d_half = z.d // 2
    copies.start(gdb.at[pl.ds(0, d_half)], gdn)
    copies.start(gdb.at[pl.ds(d_half, d_half)], gdf)
    copies.wait(*cx)
    nh, _ = norm_stats(xb[...])
    new = mm(split(nh * gain), split(ub[...]), 0, 0)
    gub[...] = gub[...] + new if accumulate else new
    copies.start(gub.at[pl.ds(0, d_half)], gun)
    copies.start(gub.at[pl.ds(d_half, d_half)], guf)
    copies.wait_all()


def ffn_bwd(z, l, last, blocks, inputs, olds):
    r = z.queries if last else z.rows
    big = lambda t=F32: pltpu.VMEM((z.d, z.d), t)
    tall = lambda t=F32: pltpu.VMEM((r, z.d), t)
    scratch = [tall(), pltpu.VMEM((2 * r, z.d), F32), big(), big(BF16), big(BF16), big(), big(BF16), big(BF16)]
    scratch += [tall(), tall(), tall(BF16), tall(BF16), tall(BF16), tall(BF16), tall(), big(), big()]
    scratch += [pltpu.VMEM((8, z.d), F32)]
    specs = [VMEM] + ([VMEM] if last else [ANY]) + [ANY] * (len(inputs) - 2)
    if not last:
        scratch += [tall()]
    h = z.d // 2
    outs = [(r, z.d), (r // 2, z.d), (r // 4, z.d), (r // 4, z.d), (8, z.d)] + [(h, z.d)] * 4
    aliases = None
    if olds is not None:
        aliases = {len(inputs) + i: 5 + i for i in range(4)}
        inputs = list(inputs) + list(olds)
        specs = specs + [ANY] * 4
    return run(
        functools.partial(ffn_bwd_kernel, z, l, last, olds is not None, blocks),
        f"ffn_bwd{l}",
        inputs,
        specs,
        outs,
        scratch,
        48,
        3 * 8 * r * z.d * z.d,
        32 << 20,
        aliases,
    )


def attn_bwd_kernel(z, l, first, last, accumulate, blocks, *refs):
    (vec, dyp, xm, pa, pb, pc, pd, *weights) = refs[: 7 + blocks]
    (x_in, q_in, kv_in, o_in, lse_in, mask) = refs[7 + blocks : 13 + blocks]
    refs = refs[13 + blocks :]
    c_ref = None
    if first:
        c_ref, refs = refs[0], refs[1:]
    if accumulate:
        olds, refs = refs[:2], refs[2:]
    if first:
        dy_out, dq_out, dkv_out, gv, gn, gf = refs[:6]
        refs = refs[6:]
    else:
        dy_out, mine, *theirs, gv, gn, gf = refs[:7]
        refs = refs[7:]
    (dyb, xmb, add, wb, wh, wl, xb, qb, kvb, ob, lseb, maskb, dyh, dyl, dqb, dkb, dvb, gb, gvb, sems) = refs
    copies = Copies(sems)
    rq = z.queries if last else z.rows
    half = rq // 2
    halves = load_halves(copies, dyp, dyb, (pa, pb, pc, pd), add)
    for i in range(2):
        here = pl.ds(i * half, half)
        halves[i].append(copies.start(xm.at[here], xmb.at[here]))
    cw = load_weight(copies, weights, wb, c_ref)
    cq = [copies.start(q_in, qb), copies.start(kv_in, kvb), copies.start(o_in, ob)]
    cq += [copies.start(lse_in, lseb), copies.start(mask, maskb)]
    cx = [copies.start(x_in, xb)]
    if accumulate:
        co = list(load_pair(copies, olds[0], olds[1], gb))
    gvb[...] = jnp.zeros_like(gvb)
    gain2 = row(vec, z.depth + l)
    for i in range(2):
        here = pl.ds(i * half, half)
        copies.wait(*halves[i])
        total = add[pl.ds(2 * i * half, half), :] + add[pl.ds((2 * i + 1) * half, half), :]
        nh, rstd = norm_stats(xmb[here, :])
        dy = dyb[here, :] + norm_back(total * gain2, nh, rstd)
        gvb[pl.ds(z.depth + l, 1), :] += z.share * jnp.sum(total * nh, axis=0, keepdims=True)
        dyb[here, :] = dy
        a, b = split(dy)
        dyh[here, :] = a
        dyl[here, :] = b
    copies.start(dyb, dy_out)
    copies.wait(*cw)
    split_into(wh, wl, wb[...])
    copies.wait(*cq)
    kh = split(kvb[:, z.k])
    vh = split(kvb[:, z.v])
    km = [keep(kh, h * HD) for h in range(z.heads)]
    dkb[...] = jnp.zeros_like(dkb)
    dvb[...] = jnp.zeros_like(dvb)
    tiles = [(0, rq)] if last else [(half, half), (0, half)]
    for start, size in tiles:
        here = pl.ds(start, size)
        do = mm((dyh[here, :], dyl[here, :]), (wh[:, z.o], wl[:, z.o]), 1, 0)
        doh = split(do)
        prod = do * ob[here, :]
        qh = split(qb[here, :])
        m_tile = maskb[...] if last else maskb[pl.ds((start // half) * z.hq, z.hq), :]
        dq = jnp.zeros((size, 256), F32)
        for h in range(z.heads):
            qm = keep(qh, h * HD)
            dm = keep(doh, HD + h * HD)
            s = scores(z, qh, kh, h, m_tile, 0 if last else z.hc)
            p = jnp.exp(s - lseb[here, h : h + 1])
            delta = jnp.sum(
                jnp.where(lanes(prod.shape, HD + h * HD), prod, 0.0), axis=-1, keepdims=True
            )
            dp = mm(dm, vh, 1, 1)
            ds = split(p * (dp - delta))
            dq = dq + mm(ds, km[h], 1, 0)
            dkb[...] += mm(ds, qm, 0, 0)
            dvb[...] += mm(split(p), dm, 0, 0)
        dqb[here, :] = dq * QSCALE
    kvb[:, 0:128] = dkb[:, 0:128]
    kvb[:, 128:256] = dkb[:, 128:256] + dvb[:, 0:128]
    kvb[:, 256:384] = dvb[:, 128:256]
    if first:
        copies.start(dqb, dq_out)
        copies.start(kvb, dkv_out)
    if accumulate:
        copies.wait(*co)
    g_out = mm((dyh[...], dyl[...]), split(ob[...]), 0, 0)
    copies.wait(*cx)
    gain = row(vec, l)
    dnb = add
    g_q = jnp.zeros((z.d, 256), F32)
    g_kv = jnp.zeros((z.d, 384), F32)
    for i in (1, 0):
        here = pl.ds(i * z.half, z.half)
        nh, rstd = norm_stats(xb[here, :])
        n = split(nh * gain)
        nc = (n[0][: z.hc], n[1][: z.hc])
        nq = (n[0][z.hc :], n[1][z.hc :]) if last else n
        qrows = pl.ds(i * z.hq, z.hq) if last else here
        dq = split(dqb[qrows, :])
        dkv = split(kvb[pl.ds(i * z.hc, z.hc), :])
        g_q = g_q + mm(nq, dq, 0, 0)
        g_kv = g_kv + mm(nc, dkv, 0, 0)
        if first:
            continue
        dn_q = mm(dq, (wh[:, z.q], wl[:, z.q]), 1, 1)
        dn_c = mm(dkv, (wh[:, z.kv], wl[:, z.kv]), 1, 1)
        if last:
            dn = jnp.concatenate([dn_c, dn_q], axis=0)
        else:
            dn = jnp.concatenate([dn_q[: z.hc] + dn_c, dn_q[z.hc :]], axis=0)
        dnb[pl.ds(i * z.half, z.half), :] = dn
        if i > 0:
            send_parts(copies, dnb, z.half, None, theirs)
        else:
            copies.start(dnb.at[here], mine)
    copies.start(gvb, gv)
    new = [
        g_kv,
        g_q[:, 0:128],
        g_q[:, 128:256] + g_out[:, 0:128],
        g_out[:, 128:256],
    ]
    at = 0
    for piece in new:
        cols = slice(at, at + piece.shape[1])
        gb[:, cols] = gb[:, cols] + piece if accumulate else piece
        at += piece.shape[1]
    d_half = z.d // 2
    copies.start(gb.at[pl.ds(0, d_half)], gn)
    copies.start(gb.at[pl.ds(d_half, d_half)], gf)
    copies.wait_all()


def attn_bwd(z, l, last, blocks, inputs, firsts, olds):
    first = l == 0
    rq = z.queries if last else z.rows
    big = lambda t=F32: pltpu.VMEM((z.d, z.d), t)
    tall = lambda t=F32: pltpu.VMEM((rq, z.d), t)
    scratch = [tall(), tall(), pltpu.VMEM((2 * z.rows, z.d), F32), big(), big(BF16), big(BF16)]
    scratch += [pltpu.VMEM((z.rows, z.d), F32), pltpu.VMEM((rq, 256), F32), pltpu.VMEM((z.context, 384), F32)]
    scratch += [pltpu.VMEM((rq, 256), F32), pltpu.VMEM((rq, 128), F32), pltpu.VMEM((z.queries, z.context), F32)]
    scratch += [tall(BF16), tall(BF16), pltpu.VMEM((rq, 256), F32)]
    scratch += [pltpu.VMEM((z.context, 256), F32), pltpu.VMEM((z.context, 256), F32), big(), pltpu.VMEM((8, z.d), F32)]
    specs = [VMEM] + [ANY] * (12 + blocks)
    h = z.d // 2
    outs = [(8, z.d), (h, z.d), (h, z.d)]
    inputs = list(inputs)
    if first:
        inputs += list(firsts)
        specs += [SMEM]
        outs = [(rq, z.d), (rq, 256), (z.context, 384)] + outs
        grads = [4, 5]
    else:
        outs = [(rq, z.d), (z.half, z.d), (z.half // 2, z.d), (z.half // 2, z.d)] + outs
        grads = [5, 6]
    aliases = None
    if olds is not None:
        aliases = {len(inputs) + i: g for i, g in enumerate(grads)}
        inputs += list(olds)
        specs += [ANY] * len(olds)
    return run(
        functools.partial(attn_bwd_kernel, z, l, first, last, olds is not None, blocks),
        f"attn_bwd{l}",
        inputs,
        specs,
        outs,
        scratch,
        48,
        3 * 2 * (4 * rq * z.d * 256 + 2 * z.context * z.d * 384 + 15 * rq * z.context * 256),
        24 << 20,
        aliases,
    )


def embed_bwd_kernel(z, accumulate, blocks, *refs):
    (c_ref, t_in, vec, feat, x_in, dy, dq, dkv, *weights) = refs[: 8 + blocks]
    refs = refs[8 + blocks :]
    if accumulate:
        old, refs = refs[0], refs[1:]
    gv, emb_out = refs[:2]
    (xb, dyb, dqb, kvb, wb, wh, wl, featb, geb, gvb, sems) = refs[2:]
    copies = Copies(sems)
    cw = load_weight(copies, weights, wb, c_ref)
    cd = [copies.start(dq, dqb), copies.start(dkv, kvb)]
    cx = [copies.start(x_in, xb), copies.start(dy, dyb)]
    cx += load_feats(copies, z, c_ref, feat, featb)
    if accumulate:
        co = copies.start(old, geb)
    gvb[...] = jnp.zeros_like(gvb)
    copies.wait(*cw)
    split_into(wh, wl, wb[...])
    copies.wait(*cd)
    copies.wait(*cx)
    gain = row(vec, 0)
    ge = 0.0
    for i in range(2):
        here = pl.ds(i * z.half, z.half)
        nh, rstd = norm_stats(xb[here, :])
        dn_q = mm(split(dqb[here, :]), (wh[:, z.q], wl[:, z.q]), 1, 1)
        dn_c = mm(split(kvb[pl.ds(i * z.hc, z.hc), :]), (wh[:, z.kv], wl[:, z.kv]), 1, 1)
        dn = jnp.concatenate([dn_q[: z.hc] + dn_c, dn_q[z.hc :]], axis=0)
        gvb[pl.ds(0, 1), :] += jnp.sum(dn * nh, axis=0, keepdims=True)
        dx = z.share * dyb[here, :] + norm_back(dn * gain, nh, rstd)
        gvb[pl.ds(2 * z.depth + 1, 1), :] += jnp.sum(dx * t_in[here, :], axis=0, keepdims=True)
        ge = ge + mm(split(dx), split(featb[here, :]), 0, 0)
    copies.start(gvb, gv)
    if accumulate:
        copies.wait(co)
        ge = geb[...] + ge
    geb[...] = ge
    copies.start(geb, emb_out)
    copies.wait_all()


def embed_bwd(z, blocks, inputs, old):
    big = lambda t=F32: pltpu.VMEM((z.d, z.d), t)
    scratch = [pltpu.VMEM((z.rows, z.d), F32), pltpu.VMEM((z.rows, z.d), F32), pltpu.VMEM((z.rows, 256), F32)]
    scratch += [pltpu.VMEM((z.context, 384), F32), big(), big(BF16), big(BF16)]
    scratch += [pltpu.VMEM((z.rows, z.feats), F32), pltpu.VMEM((z.d, z.feats), F32), pltpu.VMEM((8, z.d), F32)]
    specs = [SMEM, VMEM, VMEM] + [ANY] * (5 + blocks)
    aliases = None
    if old is not None:
        aliases = {len(inputs): 1}
        inputs = list(inputs) + [old]
        specs = specs + [ANY]
    return run(
        functools.partial(embed_bwd_kernel, z, old is not None, blocks),
        "embed_bwd",
        inputs,
        specs,
        [(8, z.d), (z.d, z.feats)],
        scratch,
        48,
        3 * 2 * (z.rows * z.d * 256 + z.context * z.d * 384 + z.rows * z.d * z.feats),
        12 << 20,
        aliases,
    )


def roll_half(x, c):
    half = x.shape[0] // 2
    return jnp.where(c == 0, x, jnp.concatenate([x[half:], x[:half]], axis=0))


def interleave(ctx, qry):
    hc, hq = ctx.shape[0] // 2, qry.shape[0] // 2
    return jnp.concatenate([ctx[:hc], qry[:hq], ctx[hc:], qry[hq:]], axis=0)


def neighbour_mask(neigh, live, context_rows, c):
    words = context_rows // 32
    col = jnp.bitwise_xor(neigh, c * (context_rows // 2))
    bit = jnp.left_shift(live, jnp.bitwise_and(col, 31))
    at = jnp.right_shift(col, 5)
    index = jnp.arange(words, dtype=jnp.int32)[None, :, None]
    word = jnp.sum(jnp.where(at[:, None, :] == index, bit[:, None, :], 0), axis=-1)
    spread = jnp.broadcast_to(word[:, :, None], word.shape + (32,)).reshape(word.shape[0], context_rows)
    shift = jnp.bitwise_and(jnp.arange(context_rows, dtype=jnp.int32), 31)
    return jnp.bitwise_and(jnp.right_shift(spread, shift[None, :]), 1).astype(F32)


def adamw(weight, grad, first, second, rate, decay, steps_taken):
    first_new = 0.9 * first + 0.1 * grad
    second_new = 0.999 * second + 0.001 * grad * grad
    first_hat = first_new / (1.0 - jnp.power(0.9, steps_taken))
    second_hat = second_new / (1.0 - jnp.power(0.999, steps_taken))
    weight_new = weight - rate * (first_hat / (jnp.sqrt(second_hat) + 1e-08) + decay * weight)
    return (weight_new, first_new, second_new)


def on_device(
    features,
    targets,
    neighbours,
    nbr_mask,
    flags,
    step_count,
    w_qkv,
    w_out,
    w_up,
    w_down,
    emb_weight,
    vectors,
    m_qkv,
    m_out,
    m_up,
    m_down,
    m_emb,
    m_vectors,
    v_qkv,
    v_out,
    v_up,
    v_down,
    v_emb,
    v_vectors,
):
    depth, d_rows = w_qkv.shape[:2]
    micros, _, rows, feats = features.shape
    queries = neighbours.shape[2]
    context = rows - queries
    width = w_qkv.shape[2] // 3
    d = d_rows * lax.axis_size("dh") * lax.axis_size("dl")
    share = 1.0 / (lax.axis_size("hh") * lax.axis_size("hl"))
    z = Sizes(d, context, queries, depth, width, feats, share)
    c = lax.axis_index("hl")
    c_arr = jnp.stack([c, lax.axis_index("dh")]).astype(jnp.int32)

    zi = lax.axis_index("dh")
    line = lax.axis_size("dh")
    near_by = line == 4

    def hop(value, step):
        return lax.ppermute(value, "dh", [(i, i ^ step) for i in range(line)])

    own_rows = jnp.concatenate([emb_weight, vectors], axis=1)
    if near_by:
        b0, b1, b2, b3 = [own_rows] + [hop(own_rows, m) for m in (1, 2, 3)]
        odd, high = jnp.bitwise_and(zi, 1) == 1, zi >= 2
        b0, b1 = jnp.where(odd, b1, b0), jnp.where(odd, b0, b1)
        b2, b3 = jnp.where(odd, b3, b2), jnp.where(odd, b2, b3)
        near = [jnp.where(high, b2, b0), jnp.where(high, b3, b1), jnp.where(high, b0, b2), jnp.where(high, b1, b3)]
        near = jnp.concatenate(near, axis=0)
        far = swap(near, "dl")
    else:
        near, far = gather_rows(own_rows)
    small = jnp.concatenate([near, far], axis=0)
    emb = small[:, :feats]
    vec = jnp.pad(small[:, feats:].T, ((0, 1), (0, 0)))
    def rows_near(block):
        return lax.all_gather(block, "dh", axis=0, tiled=True)

    blocks = []
    for l in range(depth):
        parts = [w_qkv[l][:, width:], w_qkv[l][:, :width], w_out[l]]
        blocks += [jnp.concatenate(parts, axis=1), w_up[l], w_down[l]]

    tables = []
    for m in range(micros):
        t_ctx = roll_half(targets[m, 0][:context], c)
        t_qry = roll_half(targets[m, 0][context:], c)
        t_in = interleave(t_ctx, jnp.zeros((queries,), F32))[:, None]
        flag = roll_half(flags[m, 0], c).astype(F32)
        mask = neighbour_mask(roll_half(neighbours[m, 0], c), roll_half(nbr_mask[m, 0], c), context, c)
        tables.append(dict(feat=features[m, 0], t_in=t_in, side=jnp.stack([flag, t_qry], axis=1), mask=mask))

    held, pending = [vec], []

    def beside(kernel, *transfers, ahead=(), strict=False):
        gate = after(held[0], *ahead)
        moved = [t() for t in transfers]
        outs = list(kernel(gate))
        moved = [after(x, outs[0]) for x in moved]
        held[0] = after(vec, *moved)
        for pieces in pending:
            pieces.append(swap(after(pieces[1], outs[0]), "hl"))
        pending.clear()
        if strict:
            outs[-1] = after(outs[-1], *moved)
        return (outs, *moved)

    def sent(pieces):
        held[0] = after(held[0], pieces[0])
        came[0] = pieces[1]
        pending.append(pieces)
        return pieces

    came = [None]
    near, far = [None] * len(blocks), [None] * len(blocks)

    def gather(i):
        return lambda: rows_near(blocks[i])

    def cross(i, part=None):
        if part is None:
            return lambda: swap(near[i], "dl")
        half = near[i].shape[0] // 2
        return lambda: swap(near[i][part * half : (part + 1) * half], "dl")

    def both(i):
        return near[i] if isinstance(near[i], tuple) else (near[i], far[i])

    def held_blocks(*indices):
        return tuple(len(both(i)) for i in indices)

    saved = [[None] * depth for _ in range(micros)]
    state = [None] * micros

    def attn_forward(l, m, *transfers, ahead=(), strict=False):
        t, last = tables[m], l == depth - 1

        def call(gate):
            if l == 0:
                inputs = (c_arr, t["t_in"], gate, t["feat"], emb, *both(0), t["mask"])
            else:
                inputs = (gate, state[m][0], *state[m][1], *both(3 * l), t["mask"])
            return attn_fwd(z, l, last, *held_blocks(3 * l), inputs)

        (x, q, kv, o, lse, mine, *theirs), *moved = beside(call, *transfers, ahead=ahead, strict=strict)
        saved[m][l] = dict(x=x, q=q, kv=kv, o=o, lse=lse)
        state[m] = (x, sent(head_sum(mine, theirs, came[0])))
        return moved

    def ffn_forward(l, m, *transfers, ahead=(), strict=False):
        def call(gate):
            inputs = (gate, state[m][0], *state[m][1], *both(3 * l + 1), *both(3 * l + 2))
            return ffn_fwd(z, l, l == depth - 1, held_blocks(3 * l + 1, 3 * l + 2), inputs)

        (x1, u, mine, *theirs), *moved = beside(call, *transfers, ahead=ahead, strict=strict)
        saved[m][l].update(x1=x1, u=u)
        state[m] = (x1, sent(head_sum(mine, theirs, came[0])))
        return moved

    if near_by:
        first = [blocks[0]] + [hop(blocks[0], m) for m in (1, 2, 3)]
        near[0] = tuple(first + [swap(block, "dl") for block in first])
        crossed = [jnp.concatenate([blocks[i], swap(blocks[i], "dl")], axis=0) for i in (2, 5)]
        near[2] = (rows_near(crossed[0]),)
    else:
        near[0] = gather_rows(blocks[0])
        near[2] = gather_rows(blocks[2])
    near[1] = rows_near(blocks[1])
    attn_forward(0, 0, ahead=(near[1],))
    (far[1],) = attn_forward(0, 1, cross(1), strict=True)
    (near[3],) = ffn_forward(0, 0, gather(3))
    far[3], near[4] = ffn_forward(0, 1, cross(3), gather(4))
    if near_by:
        far[4], got = attn_forward(1, 0, cross(4), lambda: rows_near(crossed[1]))
        near[5] = (got,)
        attn_forward(1, 1)
    else:
        far[4], near[5] = attn_forward(1, 0, cross(4), gather(5))
        (far[5],) = attn_forward(1, 1, cross(5), strict=True)
    ffn_forward(1, 0)
    ffn_forward(1, 1)

    g_attn, g_ffn = [None] * depth, [None] * depth
    g_vecs = []
    cot = [None] * micros

    def ffn_backward(l, m, *transfers):
        k, last = saved[m][l], l == depth - 1

        def call(gate):
            weights = (k["u"], *both(3 * l + 1), *both(3 * l + 2))
            if last:
                inputs = (gate, tables[m]["side"], k["x1"], *state[m][1], *weights)
            else:
                res, pieces = cot[m]
                inputs = (gate, res, saved[m][l + 1]["x"], k["x1"], *pieces, *weights)
            return ffn_bwd(z, l, last, held_blocks(3 * l + 1, 3 * l + 2), inputs, g_ffn[l])

        (dy, mine, t0, t1, gv, *g_ffn[l]), *moved = beside(call, *transfers)
        g_vecs.append(gv)
        cot[m] = (dy, sent(head_sum(mine, (t0, t1), came[0])))
        return moved

    def attn_backward(l, m, *transfers):
        k, t, last = saved[m][l], tables[m], l == depth - 1

        def call(gate):
            dy, pieces = cot[m]
            inputs = (gate, dy, k["x1"], *pieces, *both(3 * l), k["x"], k["q"], k["kv"], k["o"], k["lse"], t["mask"])
            firsts = (c_arr,) if l == 0 else ()
            return attn_bwd(z, l, last, *held_blocks(3 * l), inputs, firsts, g_attn[l])

        outs, *moved = beside(call, *transfers)
        if l == 0:
            *cot[m], gv, g_near, g_far = outs
            g_attn[l] = [g_near, g_far]
        else:
            dy, mine, t0, t1, gv, *g_attn[l] = outs
            cot[m] = (dy, sent(head_sum(mine, (t0, t1), came[0])))
        g_vecs.append(gv)
        return moved

    def cross_far(pair):
        return lambda: swap(pair[1], "dl")

    def reduce(part):
        return lambda: scatter_near(part)

    ffn_backward(1, 0)
    ffn_backward(1, 1)
    up1, down1 = g_ffn[1][:2], g_ffn[1][2:]
    attn_backward(1, 0)
    (got,) = attn_backward(1, 1, cross_far(up1))
    own_up1 = up1[0] + got
    packed1 = g_attn[1][:2]
    got, own_up1 = ffn_backward(0, 0, cross_far(down1), reduce(own_up1))
    own_down1 = down1[0] + got
    got, own_down1 = ffn_backward(0, 1, cross_far(packed1), reduce(own_down1))
    own_packed1 = packed1[0] + got
    up0, down0 = g_ffn[0][:2], g_ffn[0][2:]
    got, own_packed1 = attn_backward(0, 0, cross_far(up0), reduce(own_packed1))
    own_up0 = up0[0] + got
    got, own_up0 = attn_backward(0, 1, cross_far(down0), reduce(own_up0))
    own_down0 = down0[0] + got

    g_emb = [None]

    def embed_backward(m, *transfers):
        t = tables[m]

        def call(gate):
            inputs = (c_arr, t["t_in"], gate, t["feat"], saved[m][0]["x"], *cot[m], *both(0))
            return embed_bwd(z, *held_blocks(0), inputs, g_emb[0])

        (gv, g_emb[0]), *moved = beside(call, *transfers)
        g_vecs.append(gv)
        return moved

    packed0 = g_attn[0]
    got = swap(after(packed0[1], own_down0), "dl")
    own_down0 = scatter_near(own_down0)
    embed_backward(0)
    embed_backward(1)
    own_down0 = after(own_down0, g_vecs[-1])
    own_packed0 = scatter_near(packed0[0] + after(got, g_vecs[-1]))
    own = [[own_packed0, own_packed1], [own_up0, own_up1], [own_down0, own_down1]]

    owned = [
        jnp.stack([jnp.concatenate([o[:, 2 * width : 3 * width], o[:, : 2 * width]], axis=1) for o in own[0]]),
        jnp.stack([o[:, 3 * width :] for o in own[0]]),
        jnp.stack(own[1]),
        jnp.stack(own[2]),
    ]
    n_vec = vectors.shape[1]
    g_vec = sum(g_vecs[1:], g_vecs[0])
    loss_local = share * g_vec[n_vec, 0]
    g_small = jnp.concatenate([g_emb[0], g_vec[:n_vec].T], axis=1)
    own_small = near_rows(g_small[: d // 2], g_small[d // 2 :])
    if near_by:
        piece = lambda m: lax.dynamic_slice_in_dim(own_small, jnp.bitwise_xor(zi, m) * d_rows, d_rows, axis=0)
        own_small = (piece(0) + hop(piece(1), 1)) + (hop(piece(2), 2) + hop(piece(3), 3))
    else:
        own_small = scatter_near(own_small)
    own_small = own_small + swap(own_small, "hl")
    own_small = own_small + swap(own_small, "hh")
    own_emb, own_vec = own_small[:, :feats], own_small[:, feats:]
    owned += [own_emb, own_vec]

    squares = share * jnp.sum(own_small * own_small)
    for o in owned[:4]:
        squares = squares + jnp.sum(o * o)
    counted = share * jnp.sum(flags.astype(F32))
    sums = everyone_sum(jnp.stack([squares, loss_local, counted]))
    counted = jnp.maximum(sums[2], 1.0)
    loss = sums[1] / counted
    grad_norm = jnp.sqrt(sums[0]) / counted
    factor = CLIP_AT / jnp.maximum(grad_norm, CLIP_AT) / counted
    steps_taken = step_count[0].astype(F32)
    weights = (w_qkv, w_out, w_up, w_down, emb_weight, vectors)
    firsts = (m_qkv, m_out, m_up, m_down, m_emb, m_vectors)
    seconds = (v_qkv, v_out, v_up, v_down, v_emb, v_vectors)
    new_w, new_m, new_v = [], [], []
    for i in range(6):
        rate = LR_VECTOR if i == 5 else LR_MATRIX
        decay = 0.0 if i == 5 else DECAY
        result = adamw(weights[i], owned[i] * factor, firsts[i], seconds[i], rate, decay, steps_taken)
        new_w.append(result[0])
        new_m.append(result[1])
        new_v.append(result[2])
    return (loss, grad_norm, *new_w, *new_m, *new_v)


def solution(mesh):
    dp, head = mesh.shape["dp"], mesh.shape["head"]
    fine = Mesh(mesh.devices.reshape(dp // 2, 2, head // 2, 2), AXES)
    rows, cols = ("dh", "dl"), ("hh", "hl")
    data = (
        P(None, rows, None, None),
        P(None, rows, None),
        P(None, rows, None, None),
        P(None, rows, None, None),
        P(None, rows, None),
        P(),
    )
    params = (P(None, rows, cols),) * 4 + (P(rows, None),) * 2
    return jax.shard_map(
        on_device,
        mesh=fine,
        in_specs=data + params * 3,
        out_specs=(P(), P()) + params * 3,
        check_vma=False,
    )
```
